32 devices in a mesh: req: 4 (over y, x), hid: 8 (over z, core).
Axes of the slice: x: 2, y: 2, z: 4, core: 2. Of those that a mesh axis runs over, the one named last changes fastest.
Arguments:
- patches: bfloat16 [4096, 1408], P('req'), may hold values from -6 to 6
- segments: int32 [4096], P('req'), may hold values from 0 to 31, as said below
- grid_sizes: int32 [32, 2], replicated, may hold values from 0 to 32, as said below
- owners: int32 [32], replicated, may hold values from 0 to 3, as said below
- row_table: bfloat16 [32, 1408], replicated, may hold values from -3 to 3
- col_table: bfloat16 [32, 1408], replicated, may hold values from -3 to 3
- gain_attn: float32 [1408], replicated, may hold values from 0.1 to 1.9
- qkv_weight: bfloat16 [3, 1408, 1408], P(None, None, 'hid')
- out_weight: bfloat16 [1408, 1408], replicated, may hold values from -0.15625 to 0.15625
- gain_mlp: float32 [1408], replicated, may hold values from 0.1 to 1.9
- up_weight: bfloat16 [1408, 6144], P(None, 'hid'), may hold values from -0.15625 to 0.15625
- down_weight: bfloat16 [6144, 1408], P('hid'), may hold values from -0.078125 to 0.078125
- merge_weight: bfloat16 [5632, 4096], P(None, 'hid'), may hold values from -0.078125 to 0.078125
Outputs:
- returned: bfloat16 [4, 256, 4096], P('req', None, 'hid')
The draws below stay inside these ranges and needn't reach their ends.
Inputs may be any that keep to these rules, and one draw needn't show every extreme that they name: `grid_sizes`: row r holds request r's patch grid as (height, width); both are even; a request of height 0 holds no patches, and the first and the last request are never of height 0; every width is 32, 16 or 8. `owners`: every owner appears in exactly 8 entries, and its requests hold exactly 256 2x2 cells together. segments[p] is the request holding patch p: the requests' patches lie end to end in table order, each image as 2x2 cells of four consecutive patches (top left, top right, bottom left, bottom right), cells in row-major order.
All inputs are finite; a program needn't handle non-finite values.
Results may differ from the reference program's by a relative error of at most 0.018.
Values may be sent and summed in bfloat16 or wider, within the bound.
No kernel may reach another device: no remote copies, remote signals or barrier semaphores. Data moves between devices by JAX's collectives and lax.ppermute only.
A program may use at most 128 MiB of HBM per device.

```python
import math
import jax
import jax.numpy as jnp
from jax import lax

D = 1408
HEADS = 16
HEAD_DIM = 88
FF = 6144
OUTW = 4096
CELL_MOST = 16
REQ_OWN = 8
FF_DEV = 768
GROUP = 1024
TOKENS = 4096
MERGED_GROUP = 256
MERGED = 1024
REQUESTS = 32
N_REQ = 4
N_HID = 8


def request_plan(key):
    owner_count = REQUESTS // REQ_OWN
    plan_key = jax.random.fold_in(key, 101)
    key_width, key_height, key_packing, key_star = jax.random.split(plan_key, 4)
    owner_ids = jnp.arange(owner_count, dtype=jnp.int32)
    star_owner = jax.random.randint(key_star, (), 0, owner_count, dtype=jnp.int32)
    second_owner = ((star_owner + 1) % owner_count).astype(jnp.int32)
    special = (owner_ids == star_owner) | (owner_ids == second_owner)
    width_choices = jnp.array([CELL_MOST, CELL_MOST // 2, CELL_MOST // 4], dtype=jnp.int32)
    halving = jax.random.randint(key_width, (owner_count,), 0, 3, dtype=jnp.int32)
    cell_width = jnp.where(special, CELL_MOST, width_choices[halving]).astype(jnp.int32)
    height_total = (MERGED_GROUP // cell_width).astype(jnp.int32)
    height_draw = jax.random.randint(key_height, (REQ_OWN, owner_count), 1, CELL_MOST + 1, dtype=jnp.int32)
    leading = jnp.where(owner_ids == star_owner, MERGED_GROUP // CELL_MOST - 1, jnp.where(owner_ids == second_owner, 1, height_draw[0])).astype(jnp.int32)
    height_draw = jnp.concatenate([leading[None, :], height_draw[1:]], axis=0)
    steps_left = (REQ_OWN - jnp.arange(REQ_OWN, dtype=jnp.int32)).astype(jnp.int32)

    def take_height(remaining, pieces):
        wanted, left_over = pieces
        needed = (remaining + left_over - 1) // left_over
        height = jnp.minimum(remaining, jnp.maximum(wanted, needed)).astype(jnp.int32)
        return ((remaining - height).astype(jnp.int32), height)
    _, heights = lax.scan(take_height, height_total, (height_draw, steps_left))
    packing = jax.random.permutation(key_packing, REQUESTS).astype(jnp.int32)
    flat_height = jnp.transpose(heights).reshape(REQUESTS)
    flat_width = jnp.repeat(cell_width, REQ_OWN)
    flat_owner = jnp.repeat(owner_ids, REQ_OWN)
    star_lead = (star_owner * REQ_OWN).astype(jnp.int32)
    star_tail = (star_owner * REQ_OWN + 1).astype(jnp.int32)
    second_lead = (second_owner * REQ_OWN).astype(jnp.int32)
    lead_rank = jnp.where(packing == star_tail, 1, jnp.where(packing == second_lead, 2, jnp.where(packing == star_lead, 3, 0))).astype(jnp.int32)
    packed_height = flat_height[packing]
    ordinal = jnp.arange(REQUESTS, dtype=jnp.int32)
    holding = (packed_height > 0) & (lead_rank == 0)
    last_holding = jnp.max(jnp.where(holding, ordinal, -1)).astype(jnp.int32)
    scores = jnp.where(lead_rank > 0, lead_rank, jnp.where(ordinal == last_holding, 3 * REQUESTS + 8, jnp.where(holding, 4 + ordinal, 4 + REQUESTS + ordinal))).astype(jnp.int32)
    order = jnp.argsort(scores, stable=True).astype(jnp.int32)
    final = packing[order]
    grid_table = jnp.stack([2 * flat_height[final], 2 * flat_width[final]], axis=1).astype(jnp.int32)
    return (grid_table, flat_owner[final].astype(jnp.int32))


def draw_grid_sizes(key, part):
    grid_table, owner_table = request_plan(key)
    return grid_table


def draw_owners(key, part):
    grid_table, owner_table = request_plan(key)
    return owner_table


def draw_segments(key, part):
    grid_table, owner_table = request_plan(key)
    cell_count = grid_table[:, 0] // 2 * (grid_table[:, 1] // 2)
    cell_end = jnp.cumsum(cell_count).astype(jnp.int32)
    patch_index = jnp.arange(TOKENS, dtype=jnp.int32)
    return jnp.sum((4 * cell_end[None, :] <= patch_index[:, None]).astype(jnp.int32), axis=1).astype(jnp.int32)


def draw_qkv_weight(key, part):
    weights = jax.random.normal(jax.random.fold_in(key, 11), (3, D, D), jnp.float32) * (1.0 / math.sqrt(D))
    return weights.astype(jnp.bfloat16)


def steps_of(key, dims, cuts, low, high):
    factor_of = 1.0
    for position, shards_of in cuts:
        draws = jax.random.uniform(jax.random.fold_in(jax.random.fold_in(key, 6), position), (shards_of,), jnp.float32, low / len(cuts), high / len(cuts))
        factor_of = factor_of * jnp.repeat(jnp.exp(draws), dims[position] // shards_of).reshape((-1,) + (1,) * (len(dims) - 1 - position))
    return factor_of


def bell_draw(own_key, extent, deviation, reach, cuts=(), held_as=jnp.bfloat16):
    entries = jax.random.normal(own_key, extent, jnp.float32) * deviation
    if len(cuts) > 0:
        entries = steps_of(own_key, extent, cuts, -0.22, 0.18) * entries
    return jnp.clip(entries, min=-reach, max=reach).astype(held_as)


def setup_inputs(seed: int = 0) -> dict:
    seeds = jax.random.split(jax.random.key(seed), 14)
    return {
        "patches": bell_draw(seeds[0], (TOKENS, D), 1.0, 6.0, ((0, 4),)),
        "segments": draw_segments(jax.random.fold_in(seeds[13], 71), 0),
        "grid_sizes": draw_grid_sizes(jax.random.fold_in(seeds[13], 71), 0),
        "owners": draw_owners(jax.random.fold_in(seeds[13], 71), 0),
        "row_table": bell_draw(seeds[4], (2 * CELL_MOST, D), 0.5, 3.0),
        "col_table": bell_draw(seeds[5], (2 * CELL_MOST, D), 0.5, 3.0),
        "gain_attn": jnp.clip(1.0 + 0.18 * jax.random.normal(seeds[6], (D,), jnp.float32), 0.1, 1.9),
        "qkv_weight": draw_qkv_weight(jax.random.fold_in(seeds[13], 71), 0),
        "out_weight": bell_draw(seeds[8], (D, D), D ** -0.5, 0.15625),
        "gain_mlp": jnp.clip(1.0 + 0.18 * jax.random.normal(seeds[9], (D,), jnp.float32), 0.1, 1.9),
        "up_weight": bell_draw(seeds[10], (D, FF), D ** -0.5, 0.15625, ((1, 8),)),
        "down_weight": bell_draw(seeds[11], (FF, D), FF ** -0.5, 0.078125, ((0, 8),)),
        "merge_weight": bell_draw(seeds[12], (4 * D, OUTW), (4 * D) ** -0.5, 0.078125, ((1, 8),)),
    }


def stored(values):
    return lax.optimization_barrier(values.astype(jnp.bfloat16))

def layer_norm(values, gain_row):
    widened = values.astype(jnp.float32)
    centered = widened - lax.optimization_barrier(jnp.mean(widened, axis=-1, keepdims=True))
    variance = lax.optimization_barrier(jnp.mean(centered * centered, axis=-1, keepdims=True))
    return centered * lax.rsqrt(variance + 1e-06) * gain_row.astype(jnp.float32)

def request_tables(grid_sizes, owners):
    cell_count = (grid_sizes[:, 0] // 2 * (grid_sizes[:, 1] // 2)).astype(jnp.int32)
    cell_end = jnp.cumsum(cell_count).astype(jnp.int32)
    cell_start = (cell_end - cell_count).astype(jnp.int32)
    ordinal = jnp.arange(cell_count.shape[0], dtype=jnp.int32)
    earlier = (owners[:, None] == owners[None, :]) & (ordinal[None, :] < ordinal[:, None])
    preceding = lax.optimization_barrier(jnp.sum(jnp.where(earlier, cell_count[None, :], 0), axis=1)).astype(jnp.int32)
    return (cell_start, cell_end, preceding)

def attend_exact(queries, key_rows, value_rows, query_marks, key_marks):
    scores = jnp.einsum('qhe,khe->hqk', queries.astype(jnp.float32), key_rows.astype(jnp.float32)) * (1.0 / math.sqrt(HEAD_DIM))
    allowed = (query_marks[:, None] == key_marks[None, :])[None, :, :]
    scores = jnp.where(allowed, scores, -jnp.inf)
    highest = lax.optimization_barrier(jnp.max(scores, axis=2, keepdims=True))
    weights = jnp.exp(scores - highest)
    totals = lax.optimization_barrier(jnp.sum(weights, axis=2, keepdims=True))
    rounded = stored(weights).astype(jnp.float32)
    blended = jnp.einsum('hqk,khe->qhe', rounded, value_rows.astype(jnp.float32))
    return (blended / jnp.transpose(totals, (1, 0, 2))).astype(jnp.bfloat16)

def reference(patches, segments, grid_sizes, owners, row_table, col_table, gain_attn, qkv_weight, out_weight, gain_mlp, up_weight, down_weight, merge_weight):
    cell_start, cell_end, preceding = request_tables(grid_sizes, owners)
    patch_index = jnp.arange(TOKENS, dtype=jnp.int32)
    offset_in = patch_index - 4 * cell_start[segments]
    grid_cells = grid_sizes[segments, 1] // 2
    block_index = offset_in // 4
    corner = offset_in % 4
    row_place = 2 * (block_index // grid_cells) + corner // 2
    col_place = 2 * (block_index % grid_cells) + corner % 2
    embedded = stored(patches.astype(jnp.float32) + row_table[row_place].astype(jnp.float32) + col_table[col_place].astype(jnp.float32))
    normed = stored(layer_norm(embedded, gain_attn))
    queries = stored(jnp.dot(normed, qkv_weight[0], preferred_element_type=jnp.float32)).reshape(TOKENS, HEADS, HEAD_DIM)
    key_rows = stored(jnp.dot(normed, qkv_weight[1], preferred_element_type=jnp.float32)).reshape(TOKENS, HEADS, HEAD_DIM)
    value_rows = stored(jnp.dot(normed, qkv_weight[2], preferred_element_type=jnp.float32)).reshape(TOKENS, HEADS, HEAD_DIM)
    edge_rows = jnp.zeros((GROUP, HEADS, HEAD_DIM), jnp.bfloat16)
    edge_marks = jnp.full((GROUP,), -1, jnp.int32)
    all_keys = jnp.concatenate([edge_rows, key_rows, edge_rows], axis=0)
    all_values = jnp.concatenate([edge_rows, value_rows, edge_rows], axis=0)
    all_marks = jnp.concatenate([edge_marks, segments.astype(jnp.int32), edge_marks], axis=0)

    def one_group(group_index):
        first_row = (group_index * GROUP).astype(jnp.int32)
        return attend_exact(lax.dynamic_slice_in_dim(queries, first_row, GROUP, 0), lax.dynamic_slice_in_dim(all_keys, first_row, 3 * GROUP, 0), lax.dynamic_slice_in_dim(all_values, first_row, 3 * GROUP, 0), lax.dynamic_slice_in_dim(segments.astype(jnp.int32), first_row, GROUP, 0), lax.dynamic_slice_in_dim(all_marks, first_row, 3 * GROUP, 0))
    blended = lax.map(one_group, jnp.arange(N_REQ, dtype=jnp.int32)).reshape(TOKENS, D)
    attended = jnp.dot(blended, out_weight, preferred_element_type=jnp.float32)
    residual = stored(embedded.astype(jnp.float32) + attended)
    normed_mlp = stored(layer_norm(residual, gain_mlp))
    lifted = jnp.dot(normed_mlp, up_weight, preferred_element_type=jnp.float32)
    activated = stored(jax.nn.gelu(lifted, approximate=False))
    mlp_total = jnp.zeros((TOKENS, D), jnp.float32)
    for shard_index in range(N_HID):
        lower_row = shard_index * FF_DEV
        partial_sum = jnp.dot(activated[:, lower_row:lower_row + FF_DEV], down_weight[lower_row:lower_row + FF_DEV], preferred_element_type=jnp.float32)
        mlp_total = mlp_total + stored(partial_sum).astype(jnp.float32)
    output_rows = stored(residual.astype(jnp.float32) + mlp_total)
    merged = output_rows.reshape(MERGED, 4 * D)
    projected = jnp.dot(merged, merge_weight, preferred_element_type=jnp.float32).astype(jnp.bfloat16)
    merged_index = jnp.arange(MERGED, dtype=jnp.int32)
    holder = lax.optimization_barrier(jnp.sum((cell_end[None, :] <= merged_index[:, None]).astype(jnp.int32), axis=1)).astype(jnp.int32)
    target_slot = (owners[holder] * MERGED_GROUP + merged_index - cell_start[holder] + preceding[holder]).astype(jnp.int32)
    returned = jnp.zeros((MERGED, OUTW), jnp.bfloat16).at[target_slot].set(projected)
    return returned.reshape(N_REQ, MERGED_GROUP, OUTW)
```

```python
import functools
import math

import jax
import jax.numpy as jnp
from jax import lax
from jax.experimental import pallas as pl
from jax.experimental.pallas import tpu as pltpu
from jax.sharding import PartitionSpec as P

HEAD_DIM = 88
TILE = 256
LANES = 128
LOW = -1e30
VMEM_LIMIT = 56 * 1024 * 1024

NT = (((1,), (1,)), ((), ()))
TN = (((0,), (0,)), ((), ()))
TT = (((0,), (1,)), ((), ()))


def dot(left, right, dims=(((1,), (0,)), ((), ()))):
    return lax.dot_general(left, right, dims, preferred_element_type=jnp.float32)


def norm_rows(widened, gain_row):
    centered = widened - jnp.mean(widened, axis=-1, keepdims=True)
    variance = jnp.mean(centered * centered, axis=-1, keepdims=True)
    return centered * lax.rsqrt(variance + 1e-06) * gain_row


def whole(shape):
    return pl.BlockSpec(shape, lambda *_: (0,) * len(shape))


def project_kernel(
    base_ref, table_ref, patches_ref, places_ref, gain_ref, weight_ref, embedded_ref, q_ref, kv_ref
):
    rows = patches_ref.shape[0]
    width = weight_ref.shape[2]
    first = base_ref[0] + pl.program_id(0) * rows
    index = first + lax.broadcasted_iota(jnp.int32, (rows, LANES), 0)
    starts = table_ref[0:1, :]
    inside = (index >= starts) & (index < table_ref[1:2, :])
    offset = jnp.sum(jnp.where(inside, index - starts, 0), axis=1, keepdims=True)
    cells_across = jnp.sum(jnp.where(inside, table_ref[2:3, :], 0), axis=1, keepdims=True)
    shift = jnp.where(cells_across == 16, 4, jnp.where(cells_across == 8, 3, 2))
    block = offset >> 2
    corner = offset & 3
    row_place = 2 * (block >> shift) + (corner >> 1)
    col_place = 2 * (block & (cells_across - 1)) + (corner & 1)
    place_count = places_ref.shape[0]
    lane = lax.broadcasted_iota(jnp.int32, (rows, place_count), 1)
    picked = (lane == row_place) | (lane == col_place + place_count // 2)
    picked = jnp.where(picked, 1.0, 0.0).astype(jnp.bfloat16)
    embedded = (patches_ref[...].astype(jnp.float32) + dot(picked, places_ref[...])).astype(
        jnp.bfloat16
    )
    embedded_ref[...] = embedded
    normed = norm_rows(embedded.astype(jnp.float32), gain_ref[...]).astype(jnp.bfloat16)
    q_ref[...] = dot(weight_ref[0], normed, TT).astype(jnp.bfloat16)
    kv_ref[0:width, :] = dot(weight_ref[1], normed, TT).astype(jnp.bfloat16)
    kv_ref[width : 2 * width, :] = dot(weight_ref[2], normed, TT).astype(jnp.bfloat16)


def project(base, table, patches, places, gain, weight):
    rows, model = patches.shape
    width = weight.shape[2]
    return pl.pallas_call(
        project_kernel,
        grid_spec=pltpu.PrefetchScalarGridSpec(
            num_scalar_prefetch=1,
            grid=(rows // TILE,),
            in_specs=[
                whole(table.shape),
                pl.BlockSpec((TILE, model), lambda i, _: (i, 0)),
                whole(places.shape),
                whole(gain.shape),
                whole(weight.shape),
            ],
            out_specs=[
                pl.BlockSpec((TILE, model), lambda i, _: (i, 0)),
                pl.BlockSpec((width, TILE), lambda i, _: (0, i)),
                pl.BlockSpec((2 * width, TILE), lambda i, _: (0, i)),
            ],
        ),
        out_shape=[
            jax.ShapeDtypeStruct((rows, model), jnp.bfloat16),
            jax.ShapeDtypeStruct((width, rows), jnp.bfloat16),
            jax.ShapeDtypeStruct((2 * width, rows), jnp.bfloat16),
        ],
        compiler_params=pltpu.CompilerParams(vmem_limit_bytes=VMEM_LIMIT),
        cost_estimate=pl.CostEstimate(
            flops=6 * rows * model * width, bytes_accessed=4 * rows * model, transcendentals=0
        ),
    )(base, table, patches, places, gain, weight)


def attend_kernel(heads, low_ref, high_ref, base_ref, start_ref, end_ref, q_ref, *rest):
    parts, out_ref = rest[:-1], rest[-1]
    rows = q_ref.shape[1]
    width = heads * HEAD_DIM
    scale = math.log2(math.e) / math.sqrt(HEAD_DIM)
    for tile in range(rows // TILE):
        span = slice(tile * TILE, (tile + 1) * TILE)
        start = start_ref[:, span]
        end = end_ref[:, span]
        low = low_ref[tile]
        high = high_ref[tile]
        queries = [q_ref[h * HEAD_DIM : (h + 1) * HEAD_DIM, span] for h in range(heads)]
        carry = tuple(
            (
                jnp.full((1, TILE), LOW, jnp.float32),
                jnp.zeros((1, TILE), jnp.float32),
                jnp.zeros((HEAD_DIM, TILE), jnp.float32),
            )
            for _ in range(heads)
        )
        for number, part in enumerate(parts):
            base = base_ref[number]
            tiles = part.shape[1] // TILE
            first = jnp.clip((low - base) // TILE, 0, tiles)
            last = jnp.clip((high - base + TILE - 1) // TILE, 0, tiles)

            def step(place, carry, part=part, base=base, queries=queries, start=start, end=end):
                where = pl.ds(pl.multiple_of(place * TILE, TILE), TILE)
                index = base + place * TILE + lax.broadcasted_iota(jnp.int32, (TILE, TILE), 0)
                allowed = (index >= start) & (index < end)
                new = []
                for h in range(heads):
                    top, total, acc = carry[h]
                    key_rows = part[h * HEAD_DIM : (h + 1) * HEAD_DIM, where]
                    value_rows = part[width + h * HEAD_DIM : width + (h + 1) * HEAD_DIM, where]
                    scores = dot(key_rows, queries[h], TN) * scale
                    scores = jnp.where(allowed, scores, LOW)
                    higher = jnp.maximum(top, jnp.max(scores, axis=0, keepdims=True))
                    weights = jnp.exp2(scores - higher)
                    fade = jnp.exp2(top - higher)
                    total = total * fade + jnp.sum(weights, axis=0, keepdims=True)
                    acc = acc * fade + dot(value_rows, weights.astype(jnp.bfloat16))
                    new.append((higher, total, acc))
                return tuple(new)

            carry = lax.fori_loop(first, last, step, carry)
        for h in range(heads):
            _, total, acc = carry[h]
            out_ref[h * HEAD_DIM : (h + 1) * HEAD_DIM, span] = (acc / total).astype(jnp.bfloat16)


def attend(low, high, bases, start, end, queries, parts):
    width, rows = queries.shape
    heads = width // HEAD_DIM
    smem = pl.BlockSpec(memory_space=pltpu.SMEM)
    vmem = pl.BlockSpec(memory_space=pltpu.VMEM)
    return pl.pallas_call(
        functools.partial(attend_kernel, heads),
        in_specs=[smem] * 3 + [vmem] * (3 + len(parts)),
        out_specs=vmem,
        out_shape=jax.ShapeDtypeStruct((width, rows), jnp.bfloat16),
        compiler_params=pltpu.CompilerParams(vmem_limit_bytes=VMEM_LIMIT),
        cost_estimate=pl.CostEstimate(
            flops=4 * rows * rows * width,
            bytes_accessed=8 * rows * width,
            transcendentals=heads * rows * rows,
        ),
    )(low, high, bases, start, end, queries, *parts)


def mlp_kernel(
    blended_ref, embedded_ref, out_ref, gain_ref, up_ref, down_ref, residual_ref, partial_ref
):
    attended = dot(blended_ref[...], out_ref[...], TN)
    residual = (embedded_ref[...].astype(jnp.float32) + attended).astype(jnp.bfloat16)
    residual_ref[...] = residual
    normed = norm_rows(residual.astype(jnp.float32), gain_ref[...]).astype(jnp.bfloat16)
    lifted = dot(normed, up_ref[...])
    activated = (0.5 * lifted * (1.0 + lax.erf(lifted * math.sqrt(0.5)))).astype(jnp.bfloat16)
    partial_ref[...] = dot(activated, down_ref[...]).astype(jnp.bfloat16)


def mlp(blended, embedded, out_weight, gain, up_weight, down_weight):
    model, rows = blended.shape
    hidden = up_weight.shape[1]
    row_spec = pl.BlockSpec((TILE, model), lambda i: (i, 0))
    return pl.pallas_call(
        mlp_kernel,
        grid=(rows // TILE,),
        in_specs=[
            pl.BlockSpec((model, TILE), lambda i: (0, i)),
            row_spec,
            whole(out_weight.shape),
            whole(gain.shape),
            whole(up_weight.shape),
            whole(down_weight.shape),
        ],
        out_specs=[row_spec, row_spec],
        out_shape=[jax.ShapeDtypeStruct((rows, model), jnp.bfloat16)] * 2,
        compiler_params=pltpu.CompilerParams(vmem_limit_bytes=VMEM_LIMIT),
        cost_estimate=pl.CostEstimate(
            flops=2 * rows * model * (model + 2 * hidden),
            bytes_accessed=2 * (4 * rows * model + model * (model + 2 * hidden)),
            transcendentals=rows * hidden,
        ),
    )(blended, embedded, out_weight, gain, up_weight, down_weight)


def neighbour_keys(keys, band, bands):
    if bands == 4:
        across = lax.ppermute(keys, "req", [(0, 1), (1, 0), (2, 3), (3, 2)])
        along = lax.ppermute(across, "req", [(0, 2), (3, 1)])
        even = band % 2 == 0
        across_band = jnp.where(even, band + 1, band - 1)
        along_band = jnp.where(even, band - 1, band + 1)
        return (across, across_band), (along, along_band)
    after = lax.ppermute(keys, "req", [(i + 1, i) for i in range(bands - 1)])
    before = lax.ppermute(keys, "req", [(i, i + 1) for i in range(bands - 1)])
    return (before, band - 1), (after, band + 1)


def on_device(
    patches,
    segments,
    grid_sizes,
    owners,
    row_table,
    col_table,
    gain_attn,
    qkv_weight,
    out_weight,
    gain_mlp,
    up_weight,
    down_weight,
    merge_weight,
):
    rows, model = patches.shape
    bands = lax.axis_size("req")
    band = lax.axis_index("req")
    part_count = lax.axis_size("hid")
    requests = grid_sizes.shape[0]

    cells_across = grid_sizes[:, 1] // 2
    cell_count = grid_sizes[:, 0] // 2 * cells_across
    ordinal = jnp.arange(requests, dtype=jnp.int32)
    earlier = ordinal[None, :] < ordinal[:, None]
    cell_start = jnp.sum(jnp.where(earlier, cell_count[None, :], 0), axis=1)
    cell_end = cell_start + cell_count
    same_owner = earlier & (owners[:, None] == owners[None, :])
    preceding = jnp.sum(jnp.where(same_owner, cell_count[None, :], 0), axis=1)

    table = jnp.pad(
        jnp.stack([4 * cell_start, 4 * cell_end, cells_across]), ((0, 5), (0, LANES - requests))
    )
    places = jnp.concatenate([row_table, col_table], axis=0)
    base = (band * rows).astype(jnp.int32)
    embedded, queries, keys = project(
        base[None], table, patches, places, gain_attn[None, :], qkv_weight
    )

    (near, near_band), (far, far_band) = neighbour_keys(keys, band, bands)
    patch_index = base + jnp.arange(rows, dtype=jnp.int32)
    mine = (4 * cell_start[:, None] <= patch_index[None, :]) & (
        patch_index[None, :] < 4 * cell_end[:, None]
    )
    start = jnp.sum(jnp.where(mine, 4 * cell_start[:, None], 0), axis=0, keepdims=True)
    end = jnp.sum(jnp.where(mine, 4 * cell_end[:, None], 0), axis=0, keepdims=True)
    low = start[0, ::TILE]
    high = end[0, TILE - 1 :: TILE]
    beyond = 1 << 28
    part_bands = jnp.stack([band, near_band, far_band])
    bases = jnp.where((part_bands >= 0) & (part_bands < bands), part_bands * rows, beyond)
    blended = attend(low, high, bases, start, end, queries, (keys, near, far))

    gathered = lax.all_gather(blended, "hid", axis=0, tiled=True)
    residual, partial_sum = mlp(
        gathered, embedded, out_weight, gain_mlp[None, :], up_weight, down_weight
    )
    home = lax.axis_index("hid")
    summed = lax.psum_scatter(partial_sum, "hid", scatter_dimension=0, tiled=True)
    home_rows = rows // part_count
    own_residual = lax.dynamic_slice_in_dim(residual, home * home_rows, home_rows, 0)
    output_rows = (own_residual.astype(jnp.float32) + summed.astype(jnp.float32)).astype(
        jnp.bfloat16
    )
    merged = lax.all_gather(
        output_rows.reshape(home_rows // 4, 4 * model), "hid", axis=0, tiled=True
    )
    projected = jnp.dot(merged, merge_weight, preferred_element_type=jnp.float32).astype(
        jnp.bfloat16
    )

    merged_rows = projected.shape[0]
    slots = jnp.arange(merged_rows, dtype=jnp.int32)
    if bands == 4:
        shifts = (1, 2, 3)
        pieces = [projected] + [
            lax.ppermute(projected, "req", [(i, i ^ shift) for i in range(4)]) for shift in shifts
        ]
        piece_bands = [band] + [band ^ shift for shift in shifts]
    else:
        pieces = [lax.all_gather(projected, "req", axis=0, tiled=True)]
        piece_bands = [0]
    returned = jnp.zeros(projected.shape, jnp.float32)
    for piece, piece_band in zip(pieces, piece_bands):
        merged_index = piece_band * merged_rows + jnp.arange(piece.shape[0], dtype=jnp.int32)
        holding = (cell_start[None, :] <= merged_index[:, None]) & (
            merged_index[:, None] < cell_end[None, :]
        )
        holding = holding & (owners == band)[None, :]
        target = jnp.sum(
            jnp.where(holding, merged_index[:, None] + (preceding - cell_start)[None, :] + 1, 0),
            axis=1,
        )
        chosen = (target[None, :] == slots[:, None] + 1).astype(jnp.bfloat16)
        returned = returned + jnp.dot(chosen, piece, preferred_element_type=jnp.float32)
    return returned.astype(jnp.bfloat16)[None]


def solution(mesh):
    return jax.shard_map(
        on_device,
        mesh=mesh,
        in_specs=(
            P("req", None),
            P("req"),
            P(),
            P(),
            P(),
            P(),
            P(),
            P(None, None, "hid"),
            P(),
            P(),
            P(None, "hid"),
            P("hid", None),
            P(None, "hid"),
        ),
        out_specs=P("req", None, "hid"),
        check_vma=False,
    )
```

```python
import functools
import math

import jax
import jax.numpy as jnp
from jax import lax
from jax.experimental import pallas as pl
from jax.experimental.pallas import tpu as pltpu
from jax.sharding import PartitionSpec as P

HEAD_DIM = 88
TILE = 256
LANES = 128
LOW = -1e30
VMEM_LIMIT = 58 * 1024 * 1024
SHARED_VMEM = 24 * 1024 * 1024
ADD_VMEM = 8 * 1024 * 1024

NT = (((1,), (1,)), ((), ()))
TN = (((0,), (0,)), ((), ()))
TT = (((0,), (1,)), ((), ()))


def dot(left, right, dims=(((1,), (0,)), ((), ()))):
    return lax.dot_general(left, right, dims, preferred_element_type=jnp.float32)


def norm_rows(widened, gain_row):
    centered = widened - jnp.mean(widened, axis=-1, keepdims=True)
    variance = jnp.mean(centered * centered, axis=-1, keepdims=True)
    return centered * lax.rsqrt(variance + 1e-06) * gain_row


def whole(shape):
    return pl.BlockSpec(shape, lambda *_: (0,) * len(shape))


def project_kernel(
    base_ref, grid_ref, patches_ref, row_ref, col_ref, gain_ref, weight_ref, embedded_ref, q_ref, *kv_refs
):
    rows = patches_ref.shape[0]
    requests = grid_ref.shape[1]
    across = grid_ref[1:2, :] // 2
    cells = (grid_ref[0:1, :] // 2) * across
    before = lax.broadcasted_iota(jnp.int32, (requests, requests), 0)
    after = lax.broadcasted_iota(jnp.int32, (requests, requests), 1)
    earlier = jnp.where(before < after, 1.0, 0.0).astype(jnp.bfloat16)
    wide = jnp.broadcast_to(cells.astype(jnp.float32), (8, requests)).astype(jnp.bfloat16)
    starts = 4 * dot(wide, earlier)[0:1, :].astype(jnp.int32)
    index = base_ref[0] + pl.program_id(0) * rows
    index = index + lax.broadcasted_iota(jnp.int32, (rows, requests), 0)
    inside = (index >= starts) & (index < starts + 4 * cells)
    offset = jnp.sum(jnp.where(inside, index - starts, 0), axis=1, keepdims=True)
    cells_across = jnp.sum(jnp.where(inside, across, 0), axis=1, keepdims=True)
    shift = jnp.where(cells_across == 16, 4, jnp.where(cells_across == 8, 3, 2))
    block = offset >> 2
    corner = offset & 3
    row_place = 2 * (block >> shift) + (corner >> 1)
    col_place = 2 * (block & (cells_across - 1)) + (corner & 1)
    lane = lax.broadcasted_iota(jnp.int32, (rows, row_ref.shape[0]), 1)
    pick_row = jnp.where(lane == row_place, 1.0, 0.0).astype(jnp.bfloat16)
    pick_col = jnp.where(lane == col_place, 1.0, 0.0).astype(jnp.bfloat16)
    embedded = (
        patches_ref[...].astype(jnp.float32)
        + dot(pick_row, row_ref[...])
        + dot(pick_col, col_ref[...])
    ).astype(jnp.bfloat16)
    embedded_ref[...] = embedded
    normed = norm_rows(embedded.astype(jnp.float32), gain_ref[...]).astype(jnp.bfloat16)
    projected = dot(weight_ref[...], normed, NT).astype(jnp.bfloat16)
    width = q_ref.shape[0]
    q_ref[...] = projected[0:width]
    key_rows = projected[width : 2 * width]
    value_rows = projected[2 * width : 3 * width]
    for head, kv_ref in enumerate(kv_refs):
        span = slice(head * HEAD_DIM, (head + 1) * HEAD_DIM)
        kv_ref[0:HEAD_DIM, :] = key_rows[span]
        kv_ref[HEAD_DIM : 2 * HEAD_DIM, :] = value_rows[span]


def project(base, grid, patches, row_table, col_table, gain, weight):
    rows, model = patches.shape
    width = weight.shape[0] // 3
    return pl.pallas_call(
        project_kernel,
        grid_spec=pltpu.PrefetchScalarGridSpec(
            num_scalar_prefetch=1,
            grid=(rows // TILE,),
            in_specs=[
                whole(grid.shape),
                pl.BlockSpec((TILE, model), lambda i, _: (i, 0)),
                whole(row_table.shape),
                whole(col_table.shape),
                whole(gain.shape),
                whole(weight.shape),
            ],
            out_specs=[
                pl.BlockSpec((TILE, model), lambda i, _: (i, 0)),
                pl.BlockSpec((width, TILE), lambda i, _: (0, i)),
            ]
            + [pl.BlockSpec((2 * HEAD_DIM, TILE), lambda i, _: (0, i))] * (width // HEAD_DIM),
        ),
        out_shape=[
            jax.ShapeDtypeStruct((rows, model), jnp.bfloat16),
            jax.ShapeDtypeStruct((width, rows), jnp.bfloat16),
        ]
        + [jax.ShapeDtypeStruct((2 * HEAD_DIM, rows), jnp.bfloat16)] * (width // HEAD_DIM),
        compiler_params=pltpu.CompilerParams(vmem_limit_bytes=VMEM_LIMIT),
        cost_estimate=pl.CostEstimate(
            flops=6 * rows * model * width, bytes_accessed=4 * rows * model, transcendentals=0
        ),
    )(base, grid, patches, row_table, col_table, gain, weight)


def attend_kernel(taken, low_ref, high_ref, base_ref, start_ref, end_ref, q_ref, *rest):
    states, rest = rest[:taken], rest[taken:]
    count = len(rest) - (1 if taken else 3)
    parts, outs = rest[:count], rest[count:]
    rows = q_ref.shape[1]
    scale = math.log2(math.e) / math.sqrt(HEAD_DIM)
    for tile in range(rows // TILE):
        span = slice(tile * TILE, (tile + 1) * TILE)
        start = start_ref[:, span]
        end = end_ref[:, span]
        low = low_ref[tile]
        high = high_ref[tile]
        queries = q_ref[:, span]
        if taken:
            carry = tuple(state[:, span] for state in states)
        else:
            carry = (
                jnp.full((1, TILE), LOW, jnp.float32),
                jnp.zeros((1, TILE), jnp.float32),
                jnp.zeros((HEAD_DIM, TILE), jnp.float32),
            )
        for number, part in enumerate(parts):
            base = base_ref[number]
            tiles = part.shape[1] // TILE
            first = jnp.clip((low - base) // TILE, 0, tiles)
            last = jnp.clip((high - base + TILE - 1) // TILE, 0, tiles)

            def step(place, carry, part=part, base=base, queries=queries, start=start, end=end):
                where = pl.ds(pl.multiple_of(place * TILE, TILE), TILE)
                index = base + place * TILE + lax.broadcasted_iota(jnp.int32, (TILE, TILE), 0)
                allowed = (index >= start) & (index < end)
                top, total, acc = carry
                scores = dot(part[0:HEAD_DIM, where], queries, TN) * scale
                scores = jnp.where(allowed, scores, LOW)
                higher = jnp.maximum(top, jnp.max(scores, axis=0, keepdims=True))
                weights = jnp.exp2(scores - higher)
                fade = jnp.exp2(top - higher)
                total = total * fade + jnp.sum(weights, axis=0, keepdims=True)
                value_rows = part[HEAD_DIM : 2 * HEAD_DIM, where]
                acc = acc * fade + dot(value_rows, weights.astype(jnp.bfloat16))
                return higher, total, acc

            carry = lax.fori_loop(first, last, step, carry)
        if taken:
            _, total, acc = carry
            outs[0][:, span] = (acc / total).astype(jnp.bfloat16)
        else:
            for out, value in zip(outs, carry):
                out[:, span] = value


def attend(head, low, high, bases, start, end, queries, states, parts):
    rows = queries.shape[1]
    smem = pl.BlockSpec(memory_space=pltpu.SMEM)
    if states:
        shapes = [jax.ShapeDtypeStruct((HEAD_DIM, rows), jnp.bfloat16)]
    else:
        shapes = [
            jax.ShapeDtypeStruct((height, rows), jnp.float32) for height in (1, 1, HEAD_DIM)
        ]
    return pl.pallas_call(
        functools.partial(attend_kernel, len(states)),
        grid=(1,),
        in_specs=[smem] * 3
        + [whole(start.shape), whole(end.shape)]
        + [pl.BlockSpec((HEAD_DIM, rows), lambda i: (head, 0))]
        + [whole(value.shape) for value in (*states, *parts)],
        out_specs=[whole(x.shape) for x in shapes],
        out_shape=shapes,
        compiler_params=pltpu.CompilerParams(vmem_limit_bytes=VMEM_LIMIT),
        cost_estimate=pl.CostEstimate(
            flops=4 * rows * rows * HEAD_DIM,
            bytes_accessed=8 * rows * HEAD_DIM,
            transcendentals=rows * rows,
        ),
    )(low, high, bases, start, end, queries, *states, *parts)


def mlp_kernel(last, place_ref, *refs):
    blocks, refs = refs[:8], refs[8:]
    embedded_ref, gain_ref, *held = refs[:5]
    kept_ref, sent_ref = refs[5:7]
    blended_ref = refs[-1]
    height, core = place_ref[0], place_ref[1]
    width = blocks[0].shape[0]
    for k in range(4):
        for side in range(2):
            source = 2 * (height ^ k) + (core if side == 0 else 1 - core)
            blended_ref[pl.ds(pl.multiple_of(source * width, 16), width), :] = blocks[
                4 * side + k
            ][...]
    attended = dot(blended_ref[...], held[0][...], TN)
    residual = (embedded_ref[...].astype(jnp.float32) + attended).astype(jnp.bfloat16)
    rows = residual.shape[0] // 2
    normed = norm_rows(residual.astype(jnp.float32), gain_ref[...]).astype(jnp.bfloat16)
    lifted = dot(normed, held[1][...])
    activated = (0.5 * lifted * (1.0 + lax.erf(lifted * math.sqrt(0.5)))).astype(jnp.bfloat16)
    partial = dot(activated, held[2][...]).astype(jnp.bfloat16)
    for side in range(2):

        @pl.when(core == side)
        def _(side=side):
            mine = slice(side * rows, (side + 1) * rows)
            other = slice((1 - side) * rows, (2 - side) * rows)
            kept_ref[...] = partial[mine]
            sent_ref[...] = partial[other]
            if last:
                refs[7][...] = residual[mine]


def mlp(distance, place, blocks, embedded, out_weight, gain, up_weight, down_weight):
    model = embedded.shape[1]
    width = blocks[0].shape[0]
    rows = blocks[0].shape[1] // 4
    hidden = up_weight.shape[1]
    stored = (out_weight, up_weight, down_weight)
    resident = pl.BlockSpec(memory_space=pltpu.VMEM)
    last = distance == 0
    shapes = [jax.ShapeDtypeStruct((rows // 2, model), jnp.bfloat16)] * (3 if last else 2)
    return pl.pallas_call(
        functools.partial(mlp_kernel, last),
        grid_spec=pltpu.PrefetchScalarGridSpec(
            num_scalar_prefetch=1,
            grid=(1,),
            in_specs=[pl.BlockSpec((width, rows), lambda i, p: (0, p[0] ^ distance))] * 8
            + [
                pl.BlockSpec((rows, model), lambda i, p: (p[0] ^ distance, 0)),
                whole(gain.shape),
            ]
            + [resident] * 3,
            out_specs=[whole(x.shape) for x in shapes],
            scratch_shapes=[pltpu.VMEM((8 * width, rows), jnp.bfloat16)],
        ),
        out_shape=shapes,
        compiler_params=pltpu.CompilerParams(vmem_limit_bytes=SHARED_VMEM),
        cost_estimate=pl.CostEstimate(
            flops=2 * rows * model * (model + 2 * hidden),
            bytes_accessed=2 * (4 * rows * model + model * (model + 2 * hidden)),
            transcendentals=rows * hidden,
        ),
    )(place, *blocks, embedded, gain, *stored)


def add_kernel(*refs):
    total = refs[0][...].astype(jnp.float32)
    for ref in refs[1:-1]:
        total = total + ref[...].astype(jnp.float32)
    refs[-1][...] = total.astype(jnp.bfloat16)


def add(*terms):
    shape = terms[0].shape
    return pl.pallas_call(
        add_kernel,
        grid=(1,),
        in_specs=[whole(shape)] * len(terms),
        out_specs=whole(shape),
        out_shape=jax.ShapeDtypeStruct(shape, jnp.bfloat16),
        compiler_params=pltpu.CompilerParams(vmem_limit_bytes=ADD_VMEM),
        cost_estimate=pl.CostEstimate(
            flops=len(terms) * math.prod(shape),
            bytes_accessed=2 * (len(terms) + 1) * math.prod(shape),
            transcendentals=0,
        ),
    )(*terms)


def after(value, mark):
    return lax.optimization_barrier((value, mark))[0]


def along_hid(value, pairs):
    return lax.ppermute(
        value, "hid", [(2 * a + core, 2 * b + core) for a, b in pairs for core in range(2)]
    )


def swap_core(value):
    return lax.ppermute(value, "hid", [(i, i ^ 1) for i in range(8)])


NEXT = [(0, 1), (1, 0), (2, 3), (3, 2)]
SECOND = [(0, 2), (2, 0), (1, 3), (3, 1)]
MIDDLE = [(1, 2), (2, 1)]
OUTWARD = [(1, 0), (2, 3)]
INWARD = [(0, 1), (3, 2)]


def gather_line(value):
    second = along_hid(value, SECOND)
    first = along_hid(value, NEXT)
    outward = along_hid(second, OUTWARD)
    third = add(along_hid(after(value, second), MIDDLE), outward)
    return [value, first, second, third]


def across_keys(keys, bands):
    if bands == 4:
        return lax.ppermute(keys, "req", [(0, 1), (1, 0), (2, 3), (3, 2)])
    return lax.ppermute(keys, "req", [(i, i + 1) for i in range(bands - 1)])


def along_keys(keys, across, bands):
    if bands == 4:
        return lax.ppermute(across, "req", [(0, 2), (3, 1)])
    return lax.ppermute(keys, "req", [(i + 1, i) for i in range(bands - 1)])


def neighbour_bands(band, bands):
    if bands == 4:
        even = band % 2 == 0
        return jnp.where(even, band + 1, band - 1), jnp.where(even, band - 1, band + 1)
    return band - 1, band + 1


def on_device(
    patches,
    segments,
    grid_sizes,
    owners,
    row_table,
    col_table,
    gain_attn,
    qkv_weight,
    out_weight,
    gain_mlp,
    up_weight,
    down_weight,
    merge_weight,
):
    rows, model = patches.shape
    bands = lax.axis_size("req")
    band = lax.axis_index("req")
    part_count = lax.axis_size("hid")
    requests = grid_sizes.shape[0]

    cells_across = grid_sizes[:, 1] // 2
    cell_count = grid_sizes[:, 0] // 2 * cells_across
    ordinal = jnp.arange(requests, dtype=jnp.int32)
    earlier = ordinal[None, :] < ordinal[:, None]
    cell_start = jnp.sum(jnp.where(earlier, cell_count[None, :], 0), axis=1)
    cell_end = cell_start + cell_count
    same_owner = earlier & (owners[:, None] == owners[None, :])
    preceding = jnp.sum(jnp.where(same_owner, cell_count[None, :], 0), axis=1)

    base = (band * rows).astype(jnp.int32)
    embedded, queries, *keys = project(
        base[None],
        grid_sizes.T,
        patches,
        row_table,
        col_table,
        gain_attn[None, :],
        jnp.swapaxes(qkv_weight, 1, 2).reshape(-1, model),
    )

    patch_index = base + jnp.arange(rows, dtype=jnp.int32)
    mine = (4 * cell_start[:, None] <= patch_index[None, :]) & (
        patch_index[None, :] < 4 * cell_end[:, None]
    )
    start = jnp.sum(jnp.where(mine, 4 * cell_start[:, None], 0), axis=0, keepdims=True)
    end = jnp.sum(jnp.where(mine, 4 * cell_end[:, None], 0), axis=0, keepdims=True)
    low = start[0, ::TILE]
    high = end[0, TILE - 1 :: TILE]
    beyond = 1 << 28
    part_bands = jnp.stack(neighbour_bands(band, bands))
    bases = jnp.where((part_bands >= 0) & (part_bands < bands), part_bands * rows, beyond)
    near = [across_keys(own, bands) for own in keys]
    far, states = [], []
    own_base = base[None]
    for head, own in enumerate(keys):
        states.append(attend(head, low, high, own_base, start, end, queries, (), (own,)))
        near[head] = after(near[head], states[head][0])
        far.append(along_keys(own, near[head], bands))
        own_base = after(own_base, near[head])
    heads_blended = []
    for head in range(len(keys)):
        heads_blended += attend(
            head, low, high, bases, start, end, queries, states[head], (near[head], far[head])
        )

    member = lax.axis_index("hid")
    height, core = member // 2, member % 2
    place = jnp.stack([height, core]).astype(jnp.int32)
    home_cells = rows // (4 * part_count)
    merged_rows = rows // 4
    slots = jnp.arange(merged_rows, dtype=jnp.int32)

    blocks = gather_line(jnp.concatenate(heads_blended, axis=0))
    blocks = blocks + [swap_core(block) for block in blocks]
    rest = (blocks, embedded, out_weight, gain_mlp[None, :], up_weight, down_weight)

    kept, sent = mlp(3, place, *rest)
    third = add(kept, swap_core(sent))
    inward = along_hid(third, INWARD)
    middle = along_hid(third, MIDDLE)
    kept, sent = mlp(2, place, *rest)
    moved = swap_core(sent)
    kept_first, sent_first = mlp(1, after(place, third), *rest)
    second = add(kept, moved, inward)
    kept, sent, residual = mlp(0, after(place, second), *rest)
    first = add(kept_first, swap_core(sent_first))
    second = along_hid(second, SECOND)
    first = along_hid(first, NEXT)
    total = residual.astype(jnp.float32)
    for piece in (kept, swap_core(sent), middle, first, second):
        total = total + piece.astype(jnp.float32)
    output_rows = total.astype(jnp.bfloat16).reshape(home_cells, 4 * model)

    merged = gather_line(output_rows)
    returned = jnp.zeros((merged_rows, merge_weight.shape[1]), jnp.float32)
    projected = None
    for distances in ((0, 1, 2), (3,)):
        mine = [merged[k] for k in distances]
        if projected is not None:
            mine[-1] = after(mine[-1], projected)
        mine = mine + [swap_core(block) for block in mine]
        projected = jnp.dot(
            jnp.concatenate(mine, axis=0), merge_weight, preferred_element_type=jnp.float32
        ).astype(jnp.bfloat16)
        homes = jnp.stack(
            [2 * (height ^ k) + side for side in (core, 1 - core) for k in distances]
        )
        local = (
            homes[:, None] * home_cells + jnp.arange(home_cells, dtype=jnp.int32)[None, :]
        ).reshape(-1)
        if bands == 4:
            shifts = (3, 1, 2)
            pieces = [
                (lax.ppermute(projected, "req", [(i, i ^ shift) for i in range(4)]), band ^ shift)
                for shift in shifts
            ]
            pieces.append((projected, band))
            pieces = [(piece, piece_band * merged_rows + local) for piece, piece_band in pieces]
        else:
            every = jnp.arange(bands, dtype=jnp.int32)[:, None] * merged_rows + local[None, :]
            pieces = [(lax.all_gather(projected, "req", axis=0, tiled=True), every.reshape(-1))]
        for piece, merged_index in pieces:
            holding = (cell_start[None, :] <= merged_index[:, None]) & (
                merged_index[:, None] < cell_end[None, :]
            )
            holding = holding & (owners == band)[None, :]
            target = jnp.sum(
                jnp.where(holding, merged_index[:, None] + (preceding - cell_start)[None, :] + 1, 0),
                axis=1,
            )
            chosen = (target[None, :] == slots[:, None] + 1).astype(jnp.bfloat16)
            returned = returned + jnp.dot(chosen, piece, preferred_element_type=jnp.float32)
    return returned.astype(jnp.bfloat16)[None]


def solution(mesh):
    return jax.shard_map(
        on_device,
        mesh=mesh,
        in_specs=(
            P("req", None),
            P("req"),
            P(),
            P(),
            P(),
            P(),
            P(),
            P(None, None, "hid"),
            P(),
            P(),
            P(None, "hid"),
            P("hid", None),
            P(None, "hid"),
        ),
        out_specs=P("req", None, "hid"),
        check_vma=False,
    )
```

```python
import functools
import math

import jax
import jax.numpy as jnp
from jax import lax
from jax.experimental import pallas as pl
from jax.experimental.pallas import tpu as pltpu
from jax.sharding import PartitionSpec as P

HEAD_DIM = 88
TILE = 256
LANES = 128
LOW = -1e30
VMEM_LIMIT = 58 * 1024 * 1024
SHARED_VMEM = 24 * 1024 * 1024
ADD_VMEM = 8 * 1024 * 1024

NT = (((1,), (1,)), ((), ()))
TN = (((0,), (0,)), ((), ()))
TT = (((0,), (1,)), ((), ()))


def dot(left, right, dims=(((1,), (0,)), ((), ()))):
    return lax.dot_general(left, right, dims, preferred_element_type=jnp.float32)


def norm_rows(widened, gain_row):
    centered = widened - jnp.mean(widened, axis=-1, keepdims=True)
    variance = jnp.mean(centered * centered, axis=-1, keepdims=True)
    return centered * lax.rsqrt(variance + 1e-06) * gain_row


def whole(shape):
    return pl.BlockSpec(shape, lambda *_: (0,) * len(shape))


def project_kernel(
    base_ref, grid_ref, patches_ref, row_ref, col_ref, gain_ref, weight_ref, embedded_ref, q_ref, *kv_refs
):
    rows = patches_ref.shape[0]
    requests = grid_ref.shape[1]
    across = grid_ref[1:2, :] // 2
    cells = (grid_ref[0:1, :] // 2) * across
    before = lax.broadcasted_iota(jnp.int32, (requests, requests), 0)
    after = lax.broadcasted_iota(jnp.int32, (requests, requests), 1)
    earlier = jnp.where(before < after, 1.0, 0.0).astype(jnp.bfloat16)
    wide = jnp.broadcast_to(cells.astype(jnp.float32), (8, requests)).astype(jnp.bfloat16)
    starts = 4 * dot(wide, earlier)[0:1, :].astype(jnp.int32)
    index = base_ref[0] + pl.program_id(0) * rows
    index = index + lax.broadcasted_iota(jnp.int32, (rows, requests), 0)
    inside = (index >= starts) & (index < starts + 4 * cells)
    offset = jnp.sum(jnp.where(inside, index - starts, 0), axis=1, keepdims=True)
    cells_across = jnp.sum(jnp.where(inside, across, 0), axis=1, keepdims=True)
    shift = jnp.where(cells_across == 16, 4, jnp.where(cells_across == 8, 3, 2))
    block = offset >> 2
    corner = offset & 3
    row_place = 2 * (block >> shift) + (corner >> 1)
    col_place = 2 * (block & (cells_across - 1)) + (corner & 1)
    lane = lax.broadcasted_iota(jnp.int32, (rows, row_ref.shape[0]), 1)
    pick_row = jnp.where(lane == row_place, 1.0, 0.0).astype(jnp.bfloat16)
    pick_col = jnp.where(lane == col_place, 1.0, 0.0).astype(jnp.bfloat16)
    embedded = (
        patches_ref[...].astype(jnp.float32)
        + dot(pick_row, row_ref[...])
        + dot(pick_col, col_ref[...])
    ).astype(jnp.bfloat16)
    embedded_ref[...] = embedded
    normed = norm_rows(embedded.astype(jnp.float32), gain_ref[...]).astype(jnp.bfloat16)
    projected = dot(weight_ref[...], normed, NT).astype(jnp.bfloat16)
    width = q_ref.shape[0]
    q_ref[...] = projected[0:width]
    key_rows = projected[width : 2 * width]
    value_rows = projected[2 * width : 3 * width]
    for head, kv_ref in enumerate(kv_refs):
        span = slice(head * HEAD_DIM, (head + 1) * HEAD_DIM)
        kv_ref[0:HEAD_DIM, :] = key_rows[span]
        kv_ref[HEAD_DIM : 2 * HEAD_DIM, :] = value_rows[span]


def project(base, grid, patches, row_table, col_table, gain, weight):
    rows, model = patches.shape
    width = weight.shape[0] // 3
    return pl.pallas_call(
        project_kernel,
        grid_spec=pltpu.PrefetchScalarGridSpec(
            num_scalar_prefetch=1,
            grid=(rows // TILE,),
            in_specs=[
                whole(grid.shape),
                pl.BlockSpec((TILE, model), lambda i, _: (i, 0)),
                whole(row_table.shape),
                whole(col_table.shape),
                whole(gain.shape),
                whole(weight.shape),
            ],
            out_specs=[
                pl.BlockSpec((TILE, model), lambda i, _: (i, 0)),
                pl.BlockSpec((width, TILE), lambda i, _: (0, i)),
            ]
            + [pl.BlockSpec((2 * HEAD_DIM, TILE), lambda i, _: (0, i))] * (width // HEAD_DIM),
        ),
        out_shape=[
            jax.ShapeDtypeStruct((rows, model), jnp.bfloat16),
            jax.ShapeDtypeStruct((width, rows), jnp.bfloat16),
        ]
        + [jax.ShapeDtypeStruct((2 * HEAD_DIM, rows), jnp.bfloat16)] * (width // HEAD_DIM),
        compiler_params=pltpu.CompilerParams(vmem_limit_bytes=VMEM_LIMIT),
        cost_estimate=pl.CostEstimate(
            flops=6 * rows * model * width, bytes_accessed=4 * rows * model, transcendentals=0
        ),
    )(base, grid, patches, row_table, col_table, gain, weight)


def attend_kernel(heads, taken, low_ref, high_ref, base_ref, start_ref, end_ref, q_ref, *rest):
    count = base_ref.shape[0]
    states, rest = rest[: taken * heads], rest[taken * heads :]
    parts, outs = rest[: count * heads], rest[count * heads :]
    rows = q_ref.shape[1]
    scale = math.log2(math.e) / math.sqrt(HEAD_DIM)
    for tile in range(rows // TILE):
        span = slice(tile * TILE, (tile + 1) * TILE)
        start = start_ref[:, span]
        end = end_ref[:, span]
        low = low_ref[tile]
        high = high_ref[tile]
        queries = [q_ref[h * HEAD_DIM : (h + 1) * HEAD_DIM, span] for h in range(heads)]
        if taken:
            carry = tuple(
                tuple(state[:, span] for state in states[taken * h : taken * (h + 1)])
                for h in range(heads)
            )
        else:
            carry = tuple(
                (
                    jnp.full((1, TILE), LOW, jnp.float32),
                    jnp.zeros((1, TILE), jnp.float32),
                    jnp.zeros((HEAD_DIM, TILE), jnp.float32),
                )
                for _ in range(heads)
            )
        for number in range(count):
            base = base_ref[number]
            tiles = rows // TILE
            first = jnp.clip((low - base) // TILE, 0, tiles)
            last = jnp.clip((high - base + TILE - 1) // TILE, 0, tiles)

            def step(place, carry, number=number, base=base, queries=queries, start=start, end=end):
                where = pl.ds(pl.multiple_of(place * TILE, TILE), TILE)
                index = base + place * TILE + lax.broadcasted_iota(jnp.int32, (TILE, TILE), 0)
                allowed = (index >= start) & (index < end)
                new = []
                for h in range(heads):
                    part = parts[count * h + number]
                    top, total, acc = carry[h]
                    scores = dot(part[0:HEAD_DIM, where], queries[h], TN) * scale
                    scores = jnp.where(allowed, scores, LOW)
                    higher = jnp.maximum(top, jnp.max(scores, axis=0, keepdims=True))
                    weights = jnp.exp2(scores - higher)
                    fade = jnp.exp2(top - higher)
                    total = total * fade + jnp.sum(weights, axis=0, keepdims=True)
                    value_rows = part[HEAD_DIM : 2 * HEAD_DIM, where]
                    acc = acc * fade + dot(value_rows, weights.astype(jnp.bfloat16))
                    new.append((higher, total, acc))
                return tuple(new)

            carry = lax.fori_loop(first, last, step, carry)
        for h in range(heads):
            if taken:
                _, total, acc = carry[h]
                outs[h][:, span] = (acc / total).astype(jnp.bfloat16)
            else:
                for out, value in zip(outs[3 * h : 3 * h + 3], carry[h]):
                    out[:, span] = value


def attend(first_head, heads, low, high, bases, start, end, queries, states, parts):
    rows = queries.shape[1]
    smem = pl.BlockSpec(memory_space=pltpu.SMEM)
    if states:
        shapes = [jax.ShapeDtypeStruct((HEAD_DIM, rows), jnp.bfloat16)] * heads
    else:
        shapes = [
            jax.ShapeDtypeStruct((height, rows), jnp.float32) for height in (1, 1, HEAD_DIM)
        ] * heads
    return pl.pallas_call(
        functools.partial(attend_kernel, heads, len(states) // heads),
        grid=(1,),
        in_specs=[smem] * 3
        + [whole(start.shape), whole(end.shape)]
        + [pl.BlockSpec((heads * HEAD_DIM, rows), lambda i: (first_head // heads, 0))]
        + [whole(value.shape) for value in (*states, *parts)],
        out_specs=[whole(x.shape) for x in shapes],
        out_shape=shapes,
        compiler_params=pltpu.CompilerParams(vmem_limit_bytes=VMEM_LIMIT),
        cost_estimate=pl.CostEstimate(
            flops=4 * rows * rows * heads * HEAD_DIM,
            bytes_accessed=8 * rows * heads * HEAD_DIM,
            transcendentals=heads * rows * rows,
        ),
    )(low, high, bases, start, end, queries, *states, *parts)


def load_kernel(*refs):
    stored, held, token_ref, sems = refs[:3], refs[-5:-2], refs[-2], refs[-1]
    copies = [
        pltpu.make_async_copy(source, target, sems.at[i])
        for i, (source, target) in enumerate(zip(stored, held))
    ]
    for copy in copies:
        copy.start()
    token_ref[...] = jnp.zeros(token_ref.shape, token_ref.dtype)
    for copy in copies:
        copy.wait()


def load(stored, marks):
    resident = pl.BlockSpec(memory_space=pltpu.VMEM)
    token = jax.ShapeDtypeStruct((8, LANES), jnp.float32)
    *held, token = pl.pallas_call(
        load_kernel,
        in_specs=[pl.BlockSpec(memory_space=pltpu.HBM)] * 3
        + [pl.BlockSpec(memory_space=pl.ANY)] * len(marks),
        out_specs=[resident] * 4,
        out_shape=[jax.ShapeDtypeStruct(x.shape, x.dtype) for x in stored] + [token],
        scratch_shapes=[pltpu.SemaphoreType.DMA((3,))],
        compiler_params=pltpu.CompilerParams(vmem_limit_bytes=ADD_VMEM),
    )(*stored, *marks)
    return held, token


def mlp_kernel(distance, place_ref, *refs):
    *refs, sems, pieces_ref, rows_ref, blended_ref = refs
    heads = blended_ref.shape[1] // HEAD_DIM
    blocks, refs = refs[: 8 * heads], refs[8 * heads :]
    embedded_ref, gain_ref, out_ref, up_ref, down_ref, kept_ref, sent_ref = refs[:7]
    height, core = place_ref[0], place_ref[1]
    tile = rows_ref.shape[0]
    first_row = pl.multiple_of((height ^ distance) * tile, tile)
    span = pl.ds(first_row, tile)
    copies = [
        pltpu.make_async_copy(block.at[:, span], pieces_ref.at[i], sems.at[i])
        for i, block in enumerate(blocks)
    ]
    copies.append(
        pltpu.make_async_copy(embedded_ref.at[span, :], rows_ref, sems.at[len(blocks)])
    )
    for copy in copies:
        copy.start()
    for copy in copies:
        copy.wait()
    for k in range(4):
        for side in range(2):
            source = 2 * (height ^ k) + (core if side == 0 else 1 - core)
            for h in range(heads):
                where = slice(h * HEAD_DIM, (h + 1) * HEAD_DIM)
                blended_ref[source, where, :] = pieces_ref[8 * h + 4 * side + k]
    blended = blended_ref[...].reshape(-1, tile)
    attended = dot(blended, out_ref[...], TN)
    residual = (rows_ref[...].astype(jnp.float32) + attended).astype(jnp.bfloat16)
    normed = norm_rows(residual.astype(jnp.float32), gain_ref[...]).astype(jnp.bfloat16)
    lifted = dot(normed, up_ref[...])
    activated = (0.5 * lifted * (1.0 + lax.erf(lifted * math.sqrt(0.5)))).astype(jnp.bfloat16)
    partial = dot(activated, down_ref[...]).astype(jnp.bfloat16)
    rows = tile // 2
    for side in range(2):

        @pl.when(core == side)
        def _(side=side):
            mine = slice(side * rows, (side + 1) * rows)
            other = slice((1 - side) * rows, (2 - side) * rows)
            kept_ref[...] = partial[mine]
            sent_ref[...] = partial[other]
            if distance == 0:
                refs[7][...] = residual[mine]


def mlp(distance, place, blocks, embedded, gain, held):
    model = embedded.shape[1]
    heads = len(blocks) // 8
    rows = blocks[0].shape[1] // 4
    hidden = held[1].shape[1]
    away = pl.BlockSpec(memory_space=pltpu.HBM)
    shapes = [jax.ShapeDtypeStruct((rows // 2, model), jnp.bfloat16)] * (2 + (distance == 0))
    return pl.pallas_call(
        functools.partial(mlp_kernel, distance),
        grid=(1,),
        in_specs=[pl.BlockSpec(memory_space=pltpu.SMEM)]
        + [away] * (len(blocks) + 1)
        + [whole(gain.shape)]
        + [pl.BlockSpec(memory_space=pltpu.VMEM)] * 3,
        out_specs=[whole(x.shape) for x in shapes],
        out_shape=shapes,
        scratch_shapes=[
            pltpu.SemaphoreType.DMA((len(blocks) + 1,)),
            pltpu.VMEM((len(blocks), HEAD_DIM, rows), jnp.bfloat16),
            pltpu.VMEM((rows, model), jnp.bfloat16),
            pltpu.VMEM((8, heads * HEAD_DIM, rows), jnp.bfloat16),
        ],
        compiler_params=pltpu.CompilerParams(vmem_limit_bytes=SHARED_VMEM),
        cost_estimate=pl.CostEstimate(
            flops=2 * rows * model * (model + 2 * hidden),
            bytes_accessed=2 * (4 * rows * model + model * (model + 2 * hidden)),
            transcendentals=rows * hidden,
        ),
    )(place, *blocks, embedded, gain, *held)


def add_kernel(*refs):
    total = refs[0][...].astype(jnp.float32)
    for ref in refs[1:-1]:
        total = total + ref[...].astype(jnp.float32)
    refs[-1][...] = total.astype(jnp.bfloat16)


def add(*terms):
    shape = terms[0].shape
    return pl.pallas_call(
        add_kernel,
        grid=(1,),
        in_specs=[whole(shape)] * len(terms),
        out_specs=whole(shape),
        out_shape=jax.ShapeDtypeStruct(shape, jnp.bfloat16),
        compiler_params=pltpu.CompilerParams(vmem_limit_bytes=ADD_VMEM),
        cost_estimate=pl.CostEstimate(
            flops=len(terms) * math.prod(shape),
            bytes_accessed=2 * (len(terms) + 1) * math.prod(shape),
            transcendentals=0,
        ),
    )(*terms)


def after(value, mark):
    return lax.optimization_barrier((value, mark))[0]


def along_hid(value, pairs):
    return lax.ppermute(
        value, "hid", [(2 * a + core, 2 * b + core) for a, b in pairs for core in range(2)]
    )


def swap_core(value):
    return lax.ppermute(value, "hid", [(i, i ^ 1) for i in range(8)])


NEXT = [(0, 1), (1, 0), (2, 3), (3, 2)]
SECOND = [(0, 2), (2, 0), (1, 3), (3, 1)]
MIDDLE = [(1, 2), (2, 1)]
OUTWARD = [(1, 0), (2, 3)]
INWARD = [(0, 1), (3, 2)]


def gather_line(value, mark=None):
    second = along_hid(value, SECOND)
    first = along_hid(value, NEXT)
    passed, kept = (second, after(value, second))
    if mark is not None:
        passed, kept = after(passed, mark), after(kept, mark)
    third = add(along_hid(kept, MIDDLE), along_hid(passed, OUTWARD))
    return [value, first, second, third]


def across_keys(keys, bands):
    if bands == 4:
        return lax.ppermute(keys, "req", [(0, 1), (1, 0), (2, 3), (3, 2)])
    return lax.ppermute(keys, "req", [(i, i + 1) for i in range(bands - 1)])


def along_keys(keys, across, bands):
    if bands == 4:
        return lax.ppermute(across, "req", [(0, 2), (3, 1)])
    return lax.ppermute(keys, "req", [(i + 1, i) for i in range(bands - 1)])


def neighbour_bands(band, bands):
    if bands == 4:
        even = band % 2 == 0
        return jnp.where(even, band + 1, band - 1), jnp.where(even, band - 1, band + 1)
    return band - 1, band + 1


def on_device(
    patches,
    segments,
    grid_sizes,
    owners,
    row_table,
    col_table,
    gain_attn,
    qkv_weight,
    out_weight,
    gain_mlp,
    up_weight,
    down_weight,
    merge_weight,
):
    rows, model = patches.shape
    bands = lax.axis_size("req")
    band = lax.axis_index("req")
    part_count = lax.axis_size("hid")
    requests = grid_sizes.shape[0]

    cells_across = grid_sizes[:, 1] // 2
    cell_count = grid_sizes[:, 0] // 2 * cells_across
    ordinal = jnp.arange(requests, dtype=jnp.int32)
    earlier = ordinal[None, :] < ordinal[:, None]
    cell_start = jnp.sum(jnp.where(earlier, cell_count[None, :], 0), axis=1)
    cell_end = cell_start + cell_count
    same_owner = earlier & (owners[:, None] == owners[None, :])
    preceding = jnp.sum(jnp.where(same_owner, cell_count[None, :], 0), axis=1)

    base = (band * rows).astype(jnp.int32)
    embedded, queries, *keys = project(
        base[None],
        grid_sizes.T,
        patches,
        row_table,
        col_table,
        gain_attn,
        jnp.swapaxes(qkv_weight, 1, 2).reshape(-1, model),
    )

    patch_index = base + jnp.arange(rows, dtype=jnp.int32)
    mine = (4 * cell_start[:, None] <= patch_index[None, :]) & (
        patch_index[None, :] < 4 * cell_end[:, None]
    )
    start = jnp.sum(jnp.where(mine, 4 * cell_start[:, None], 0), axis=0, keepdims=True)
    end = jnp.sum(jnp.where(mine, 4 * cell_end[:, None], 0), axis=0, keepdims=True)
    low = start[0, ::TILE]
    high = end[0, TILE - 1 :: TILE]
    beyond = 1 << 28
    part_bands = jnp.stack(neighbour_bands(band, bands))
    bases = jnp.where((part_bands >= 0) & (part_bands < bands), part_bands * rows, beyond)
    near = [across_keys(own, bands) for own in keys]
    heads = len(keys)
    states = attend(0, heads, low, high, base[None], start, end, queries, (), keys)
    near[0] = after(near[0], states[0])
    far = [along_keys(own, across, bands) for own, across in zip(keys, near)]
    blended = []
    for head in range(heads):
        blended += attend(
            head,
            1,
            low,
            high,
            bases,
            start,
            end,
            queries,
            states[3 * head : 3 * head + 3],
            (near[head], far[head]),
        )

    member = lax.axis_index("hid")
    height, core = member // 2, member % 2
    place = jnp.stack([height, core]).astype(jnp.int32)
    home_cells = rows // (4 * part_count)
    merged_rows = rows // 4
    slots = jnp.arange(merged_rows, dtype=jnp.int32)

    gain_row = gain_mlp[None, :]
    held, token = load((out_weight, up_weight, down_weight), (place, gain_row, blended[-1]))
    blocks = []
    for head, piece in enumerate(blended):
        piece = gather_line(piece, token if head == heads - 1 else None)
        blocks += piece + [swap_core(block) for block in piece]
    rest = (blocks, embedded, gain_row, held)

    kept, sent = mlp(3, place, *rest)
    third = add(kept, swap_core(sent))
    inward = along_hid(third, INWARD)
    middle = along_hid(third, MIDDLE)
    kept, sent = mlp(2, after(place, third), *rest)
    moved = swap_core(sent)
    kept_first, sent_first = mlp(1, after(place, kept), *rest)
    second = add(kept, moved, after(inward, kept_first))
    kept, sent, residual = mlp(0, after(place, second), *rest)
    first = add(kept_first, swap_core(sent_first))
    second = along_hid(second, SECOND)
    first = along_hid(first, NEXT)
    total = residual.astype(jnp.float32)
    for piece in (kept, swap_core(sent), middle, first, second):
        total = total + piece.astype(jnp.float32)
    output_rows = total.astype(jnp.bfloat16).reshape(home_cells, 4 * model)

    def project_merged(blocks):
        blocks = blocks + [swap_core(block) for block in blocks]
        return jnp.dot(
            jnp.concatenate(blocks, axis=0), merge_weight, preferred_element_type=jnp.float32
        ).astype(jnp.bfloat16)

    *nearer, third = gather_line(output_rows)
    most = project_merged(nearer)
    last = project_merged([after(third, most)])
    routed = []
    for projected, distances in ((most, (0, 1, 2)), (last, (3,))):
        homes = jnp.stack(
            [2 * (height ^ k) + side for side in (core, 1 - core) for k in distances]
        )
        local = (
            homes[:, None] * home_cells + jnp.arange(home_cells, dtype=jnp.int32)[None, :]
        ).reshape(-1)
        if bands == 4:
            routed += [
                (lax.ppermute(projected, "req", [(i, i ^ shift) for i in range(4)]), band ^ shift, local)
                for shift in (3, 1, 2)
            ]
            routed.append((projected, band, local))
        else:
            every = jnp.arange(bands, dtype=jnp.int32)[:, None] * merged_rows + local[None, :]
            routed.append(
                (lax.all_gather(projected, "req", axis=0, tiled=True), 0, every.reshape(-1))
            )
    returned = jnp.zeros((merged_rows, merge_weight.shape[1]), jnp.float32)
    for piece, piece_band, local in routed:
        merged_index = piece_band * merged_rows + local
        holding = (cell_start[None, :] <= merged_index[:, None]) & (
            merged_index[:, None] < cell_end[None, :]
        )
        holding = holding & (owners == band)[None, :]
        target = jnp.sum(
            jnp.where(holding, merged_index[:, None] + (preceding - cell_start)[None, :] + 1, 0),
            axis=1,
        )
        chosen = (target[None, :] == slots[:, None] + 1).astype(jnp.bfloat16)
        piece = after(piece, last)
        returned = returned + jnp.dot(chosen, piece, preferred_element_type=jnp.float32)
    return returned.astype(jnp.bfloat16)[None]


def solution(mesh):
    return jax.shard_map(
        on_device,
        mesh=mesh,
        in_specs=(
            P("req", None),
            P("req"),
            P(),
            P(),
            P(),
            P(),
            P(),
            P(None, None, "hid"),
            P(),
            P(),
            P(None, "hid"),
            P("hid", None),
            P(None, "hid"),
        ),
        out_specs=P("req", None, "hid"),
        check_vma=False,
    )
```

```python
import functools
import math

import jax
import jax.numpy as jnp
from jax import lax
from jax.experimental import pallas as pl
from jax.experimental.pallas import tpu as pltpu
from jax.sharding import PartitionSpec as P

HEAD_DIM = 88
TILE = 256
LANES = 128
LOW = -1e30
VMEM_LIMIT = 58 * 1024 * 1024
SHARED_VMEM = 24 * 1024 * 1024
ADD_VMEM = 8 * 1024 * 1024

NT = (((1,), (1,)), ((), ()))
TN = (((0,), (0,)), ((), ()))
TT = (((0,), (1,)), ((), ()))


def dot(left, right, dims=(((1,), (0,)), ((), ()))):
    return lax.dot_general(left, right, dims, preferred_element_type=jnp.float32)


def norm_rows(widened, gain_row):
    centered = widened - jnp.mean(widened, axis=-1, keepdims=True)
    variance = jnp.mean(centered * centered, axis=-1, keepdims=True)
    return centered * lax.rsqrt(variance + 1e-06) * gain_row


def whole(shape):
    return pl.BlockSpec(shape, lambda *_: (0,) * len(shape))


def project_kernel(
    base_ref, grid_ref, patches_ref, row_ref, col_ref, gain_ref, weight_ref, embedded_ref, q_ref, *kv_refs
):
    rows = patches_ref.shape[0]
    requests = grid_ref.shape[1]
    across = grid_ref[1:2, :] // 2
    cells = (grid_ref[0:1, :] // 2) * across
    before = lax.broadcasted_iota(jnp.int32, (requests, requests), 0)
    after = lax.broadcasted_iota(jnp.int32, (requests, requests), 1)
    earlier = jnp.where(before < after, 1.0, 0.0).astype(jnp.bfloat16)
    wide = jnp.broadcast_to(cells.astype(jnp.float32), (8, requests)).astype(jnp.bfloat16)
    starts = 4 * dot(wide, earlier)[0:1, :].astype(jnp.int32)
    index = base_ref[0] + pl.program_id(0) * rows
    index = index + lax.broadcasted_iota(jnp.int32, (rows, requests), 0)
    inside = (index >= starts) & (index < starts + 4 * cells)
    offset = jnp.sum(jnp.where(inside, index - starts, 0), axis=1, keepdims=True)
    cells_across = jnp.sum(jnp.where(inside, across, 0), axis=1, keepdims=True)
    shift = jnp.where(cells_across == 16, 4, jnp.where(cells_across == 8, 3, 2))
    block = offset >> 2
    corner = offset & 3
    row_place = 2 * (block >> shift) + (corner >> 1)
    col_place = 2 * (block & (cells_across - 1)) + (corner & 1)
    lane = lax.broadcasted_iota(jnp.int32, (rows, row_ref.shape[0]), 1)
    pick_row = jnp.where(lane == row_place, 1.0, 0.0).astype(jnp.bfloat16)
    pick_col = jnp.where(lane == col_place, 1.0, 0.0).astype(jnp.bfloat16)
    embedded = (
        patches_ref[...].astype(jnp.float32)
        + dot(pick_row, row_ref[...])
        + dot(pick_col, col_ref[...])
    ).astype(jnp.bfloat16)
    embedded_ref[...] = embedded
    normed = norm_rows(embedded.astype(jnp.float32), gain_ref[...]).astype(jnp.bfloat16)
    projected = dot(weight_ref[...], normed, NT).astype(jnp.bfloat16)
    width = q_ref.shape[0]
    q_ref[...] = projected[0:width]
    key_rows = projected[width : 2 * width]
    value_rows = projected[2 * width : 3 * width]
    for head, kv_ref in enumerate(kv_refs):
        span = slice(head * HEAD_DIM, (head + 1) * HEAD_DIM)
        kv_ref[0:HEAD_DIM, :] = key_rows[span]
        kv_ref[HEAD_DIM : 2 * HEAD_DIM, :] = value_rows[span]


def project(base, grid, patches, row_table, col_table, gain, weight):
    rows, model = patches.shape
    width = weight.shape[0] // 3
    return pl.pallas_call(
        project_kernel,
        grid_spec=pltpu.PrefetchScalarGridSpec(
            num_scalar_prefetch=1,
            grid=(rows // 512,),
            in_specs=[
                whole(grid.shape),
                pl.BlockSpec((512, model), lambda i, _: (i, 0)),
                whole(row_table.shape),
                whole(col_table.shape),
                whole(gain.shape),
                whole(weight.shape),
            ],
            out_specs=[
                pl.BlockSpec((512, model), lambda i, _: (i, 0)),
                pl.BlockSpec((width, 512), lambda i, _: (0, i)),
            ]
            + [pl.BlockSpec((2 * HEAD_DIM, 512), lambda i, _: (0, i))] * (width // HEAD_DIM),
        ),
        out_shape=[
            jax.ShapeDtypeStruct((rows, model), jnp.bfloat16),
            jax.ShapeDtypeStruct((width, rows), jnp.bfloat16),
        ]
        + [jax.ShapeDtypeStruct((2 * HEAD_DIM, rows), jnp.bfloat16)] * (width // HEAD_DIM),
        compiler_params=pltpu.CompilerParams(vmem_limit_bytes=VMEM_LIMIT),
        cost_estimate=pl.CostEstimate(
            flops=6 * rows * model * width, bytes_accessed=4 * rows * model, transcendentals=0
        ),
    )(base, grid, patches, row_table, col_table, gain, weight)


def attend_kernel(heads, taken, low_ref, high_ref, base_ref, start_ref, end_ref, q_ref, *rest):
    count = base_ref.shape[0]
    states, rest = rest[: taken * heads], rest[taken * heads :]
    parts, outs = rest[: count * heads], rest[count * heads :]
    rows = q_ref.shape[1]
    scale = math.log2(math.e) / math.sqrt(HEAD_DIM)
    for tile in range(rows // TILE):
        span = slice(tile * TILE, (tile + 1) * TILE)
        start = start_ref[:, span]
        end = end_ref[:, span]
        low = low_ref[tile]
        high = high_ref[tile]
        queries = [q_ref[h * HEAD_DIM : (h + 1) * HEAD_DIM, span] for h in range(heads)]
        if taken:
            carry = tuple(
                tuple(state[:, span] for state in states[taken * h : taken * (h + 1)])
                for h in range(heads)
            )
        else:
            carry = tuple(
                (
                    jnp.full((1, TILE), LOW, jnp.float32),
                    jnp.zeros((1, TILE), jnp.float32),
                    jnp.zeros((HEAD_DIM, TILE), jnp.float32),
                )
                for _ in range(heads)
            )
        for number in range(count):
            base = base_ref[number]
            tiles = rows // TILE
            first = jnp.clip((low - base) // TILE, 0, tiles)
            last = jnp.clip((high - base + TILE - 1) // TILE, 0, tiles)

            def step(place, carry, number=number, base=base, queries=queries, start=start, end=end):
                where = pl.ds(pl.multiple_of(place * TILE, TILE), TILE)
                index = base + place * TILE + lax.broadcasted_iota(jnp.int32, (TILE, TILE), 0)
                allowed = (index >= start) & (index < end)
                new = []
                for h in range(heads):
                    part = parts[count * h + number]
                    top, total, acc = carry[h]
                    scores = dot(part[0:HEAD_DIM, where], queries[h], TN) * scale
                    scores = jnp.where(allowed, scores, LOW)
                    higher = jnp.maximum(top, jnp.max(scores, axis=0, keepdims=True))
                    weights = jnp.exp2(scores - higher)
                    fade = jnp.exp2(top - higher)
                    total = total * fade + jnp.sum(weights, axis=0, keepdims=True)
                    value_rows = part[HEAD_DIM : 2 * HEAD_DIM, where]
                    acc = acc * fade + dot(value_rows, weights.astype(jnp.bfloat16))
                    new.append((higher, total, acc))
                return tuple(new)

            carry = lax.fori_loop(first, last, step, carry)
        for h in range(heads):
            if taken:
                _, total, acc = carry[h]
                outs[h][:, span] = (acc / total).astype(jnp.bfloat16)
            else:
                for out, value in zip(outs[3 * h : 3 * h + 3], carry[h]):
                    out[:, span] = value


def attend(first_head, heads, low, high, bases, start, end, queries, states, parts):
    rows = queries.shape[1]
    smem = pl.BlockSpec(memory_space=pltpu.SMEM)
    if states:
        shapes = [jax.ShapeDtypeStruct((HEAD_DIM, rows), jnp.bfloat16)] * heads
    else:
        shapes = [
            jax.ShapeDtypeStruct((height, rows), jnp.float32) for height in (1, 1, HEAD_DIM)
        ] * heads
    return pl.pallas_call(
        functools.partial(attend_kernel, heads, len(states) // heads),
        grid=(1,),
        in_specs=[smem] * 3
        + [whole(start.shape), whole(end.shape)]
        + [pl.BlockSpec((heads * HEAD_DIM, rows), lambda i: (first_head // heads, 0))]
        + [whole(value.shape) for value in (*states, *parts)],
        out_specs=[whole(x.shape) for x in shapes],
        out_shape=shapes,
        compiler_params=pltpu.CompilerParams(vmem_limit_bytes=VMEM_LIMIT),
        cost_estimate=pl.CostEstimate(
            flops=4 * rows * rows * heads * HEAD_DIM,
            bytes_accessed=8 * rows * heads * HEAD_DIM,
            transcendentals=heads * rows * rows,
        ),
    )(low, high, bases, start, end, queries, *states, *parts)


def load_kernel(*refs):
    stored, held, token_ref, sems = refs[:3], refs[-5:-2], refs[-2], refs[-1]
    copies = [
        pltpu.make_async_copy(source, target, sems.at[i])
        for i, (source, target) in enumerate(zip(stored, held))
    ]
    for copy in copies:
        copy.start()
    token_ref[...] = jnp.zeros(token_ref.shape, token_ref.dtype)
    for copy in copies:
        copy.wait()


def load(stored, marks):
    resident = pl.BlockSpec(memory_space=pltpu.VMEM)
    token = jax.ShapeDtypeStruct((8, LANES), jnp.float32)
    *held, token = pl.pallas_call(
        load_kernel,
        in_specs=[pl.BlockSpec(memory_space=pltpu.HBM)] * 3
        + [pl.BlockSpec(memory_space=pl.ANY)] * len(marks),
        out_specs=[resident] * 4,
        out_shape=[jax.ShapeDtypeStruct(x.shape, x.dtype) for x in stored] + [token],
        scratch_shapes=[pltpu.SemaphoreType.DMA((3,))],
        compiler_params=pltpu.CompilerParams(vmem_limit_bytes=ADD_VMEM),
    )(*stored, *marks)
    return held, token


def mlp_kernel(distance, place_ref, *refs):
    *refs, sems, pieces_ref, rows_ref, blended_ref = refs
    heads = blended_ref.shape[1] // HEAD_DIM
    blocks, refs = refs[: 8 * heads], refs[8 * heads :]
    embedded_ref, gain_ref, out_ref, up_ref, down_ref, kept_ref, sent_ref = refs[:7]
    height, core = place_ref[0], place_ref[1]
    tile = rows_ref.shape[0]
    first_row = pl.multiple_of((height ^ distance) * tile, tile)
    span = pl.ds(first_row, tile)
    copies = [
        pltpu.make_async_copy(block.at[:, span], pieces_ref.at[i], sems.at[i])
        for i, block in enumerate(blocks)
    ]
    copies.append(
        pltpu.make_async_copy(embedded_ref.at[span, :], rows_ref, sems.at[len(blocks)])
    )
    for copy in copies:
        copy.start()
    for copy in copies:
        copy.wait()
    for k in range(4):
        for side in range(2):
            source = 2 * (height ^ k) + (core if side == 0 else 1 - core)
            for h in range(heads):
                where = slice(h * HEAD_DIM, (h + 1) * HEAD_DIM)
                blended_ref[source, where, :] = pieces_ref[8 * h + 4 * side + k]
    blended = blended_ref[...].reshape(-1, tile)
    attended = dot(blended, out_ref[...], TN)
    residual = (rows_ref[...].astype(jnp.float32) + attended).astype(jnp.bfloat16)
    normed = norm_rows(residual.astype(jnp.float32), gain_ref[...]).astype(jnp.bfloat16)
    lifted = dot(normed, up_ref[...])
    activated = (0.5 * lifted * (1.0 + lax.erf(lifted * math.sqrt(0.5)))).astype(jnp.bfloat16)
    partial = dot(activated, down_ref[...]).astype(jnp.bfloat16)
    rows = tile // 2
    for side in range(2):

        @pl.when(core == side)
        def _(side=side):
            mine = slice(side * rows, (side + 1) * rows)
            other = slice((1 - side) * rows, (2 - side) * rows)
            kept_ref[...] = partial[mine]
            sent_ref[...] = partial[other]
            if distance == 0:
                refs[7][...] = residual[mine]


def mlp(distance, place, blocks, embedded, gain, held):
    model = embedded.shape[1]
    heads = len(blocks) // 8
    rows = blocks[0].shape[1] // 4
    hidden = held[1].shape[1]
    away = pl.BlockSpec(memory_space=pltpu.HBM)
    shapes = [jax.ShapeDtypeStruct((rows // 2, model), jnp.bfloat16)] * (2 + (distance == 0))
    return pl.pallas_call(
        functools.partial(mlp_kernel, distance),
        grid=(1,),
        in_specs=[pl.BlockSpec(memory_space=pltpu.SMEM)]
        + [away] * (len(blocks) + 1)
        + [whole(gain.shape)]
        + [pl.BlockSpec(memory_space=pltpu.VMEM)] * 3,
        out_specs=[whole(x.shape) for x in shapes],
        out_shape=shapes,
        scratch_shapes=[
            pltpu.SemaphoreType.DMA((len(blocks) + 1,)),
            pltpu.VMEM((len(blocks), HEAD_DIM, rows), jnp.bfloat16),
            pltpu.VMEM((rows, model), jnp.bfloat16),
            pltpu.VMEM((8, heads * HEAD_DIM, rows), jnp.bfloat16),
        ],
        compiler_params=pltpu.CompilerParams(vmem_limit_bytes=SHARED_VMEM),
        cost_estimate=pl.CostEstimate(
            flops=2 * rows * model * (model + 2 * hidden),
            bytes_accessed=2 * (4 * rows * model + model * (model + 2 * hidden)),
            transcendentals=rows * hidden,
        ),
    )(place, *blocks, embedded, gain, *held)


def add_kernel(*refs):
    total = refs[0][...].astype(jnp.float32)
    for ref in refs[1:-1]:
        total = total + ref[...].astype(jnp.float32)
    refs[-1][...] = total.astype(jnp.bfloat16)


def add(*terms):
    shape = terms[0].shape
    return pl.pallas_call(
        add_kernel,
        grid=(1,),
        in_specs=[whole(shape)] * len(terms),
        out_specs=whole(shape),
        out_shape=jax.ShapeDtypeStruct(shape, jnp.bfloat16),
        compiler_params=pltpu.CompilerParams(vmem_limit_bytes=ADD_VMEM),
        cost_estimate=pl.CostEstimate(
            flops=len(terms) * math.prod(shape),
            bytes_accessed=2 * (len(terms) + 1) * math.prod(shape),
            transcendentals=0,
        ),
    )(*terms)


def after(value, mark):
    return lax.optimization_barrier((value, mark))[0]


def along_hid(value, pairs):
    return lax.ppermute(
        value, "hid", [(2 * a + core, 2 * b + core) for a, b in pairs for core in range(2)]
    )


def swap_core(value):
    return lax.ppermute(value, "hid", [(i, i ^ 1) for i in range(8)])


NEXT = [(0, 1), (1, 0), (2, 3), (3, 2)]
SECOND = [(0, 2), (2, 0), (1, 3), (3, 1)]
MIDDLE = [(1, 2), (2, 1)]
OUTWARD = [(1, 0), (2, 3)]
INWARD = [(0, 1), (3, 2)]


def gather_line(value, mark=None):
    second = along_hid(value, SECOND)
    first = along_hid(value, NEXT)
    passed, kept = (second, after(value, second))
    if mark is not None:
        passed, kept = after(passed, mark), after(kept, mark)
    third = add(along_hid(kept, MIDDLE), along_hid(passed, OUTWARD))
    return [value, first, second, third]


def across_keys(keys, bands):
    if bands == 4:
        return lax.ppermute(keys, "req", [(0, 1), (1, 0), (2, 3), (3, 2)])
    return lax.ppermute(keys, "req", [(i, i + 1) for i in range(bands - 1)])


def along_keys(keys, across, bands):
    if bands == 4:
        return lax.ppermute(across, "req", [(0, 2), (3, 1)])
    return lax.ppermute(keys, "req", [(i + 1, i) for i in range(bands - 1)])


def neighbour_bands(band, bands):
    if bands == 4:
        even = band % 2 == 0
        return jnp.where(even, band + 1, band - 1), jnp.where(even, band - 1, band + 1)
    return band - 1, band + 1


def on_device(
    patches,
    segments,
    grid_sizes,
    owners,
    row_table,
    col_table,
    gain_attn,
    qkv_weight,
    out_weight,
    gain_mlp,
    up_weight,
    down_weight,
    merge_weight,
):
    rows, model = patches.shape
    bands = lax.axis_size("req")
    band = lax.axis_index("req")
    part_count = lax.axis_size("hid")
    requests = grid_sizes.shape[0]

    cells_across = grid_sizes[:, 1] // 2
    cell_count = grid_sizes[:, 0] // 2 * cells_across
    ordinal = jnp.arange(requests, dtype=jnp.int32)
    earlier = ordinal[None, :] < ordinal[:, None]
    cell_start = jnp.sum(jnp.where(earlier, cell_count[None, :], 0), axis=1)
    cell_end = cell_start + cell_count
    same_owner = earlier & (owners[:, None] == owners[None, :])
    preceding = jnp.sum(jnp.where(same_owner, cell_count[None, :], 0), axis=1)

    base = (band * rows).astype(jnp.int32)
    embedded, queries, *keys = project(
        base[None],
        grid_sizes.T,
        patches,
        row_table,
        col_table,
        gain_attn,
        jnp.swapaxes(qkv_weight, 1, 2).reshape(-1, model),
    )

    patch_index = base + jnp.arange(rows, dtype=jnp.int32)
    mine = (4 * cell_start[:, None] <= patch_index[None, :]) & (
        patch_index[None, :] < 4 * cell_end[:, None]
    )
    start = jnp.sum(jnp.where(mine, 4 * cell_start[:, None], 0), axis=0, keepdims=True)
    end = jnp.sum(jnp.where(mine, 4 * cell_end[:, None], 0), axis=0, keepdims=True)
    low = start[0, ::TILE]
    high = end[0, TILE - 1 :: TILE]
    beyond = 1 << 28
    part_bands = jnp.stack(neighbour_bands(band, bands))
    bases = jnp.where((part_bands >= 0) & (part_bands < bands), part_bands * rows, beyond)
    near = [across_keys(own, bands) for own in keys]
    heads = len(keys)
    states = attend(0, heads, low, high, base[None], start, end, queries, (), keys)
    near[0] = after(near[0], states[0])
    far = [along_keys(own, across, bands) for own, across in zip(keys, near)]
    blended = []
    for head in range(heads):
        blended += attend(
            head,
            1,
            low,
            high,
            bases,
            start,
            end,
            queries,
            states[3 * head : 3 * head + 3],
            (near[head], far[head]),
        )

    member = lax.axis_index("hid")
    height, core = member // 2, member % 2
    place = jnp.stack([height, core]).astype(jnp.int32)
    home_cells = rows // (4 * part_count)
    merged_rows = rows // 4
    slots = jnp.arange(merged_rows, dtype=jnp.int32)

    gain_row = gain_mlp[None, :]
    held, token = load((out_weight, up_weight, down_weight), (place, gain_row, blended[-1]))
    blocks = []
    for head, piece in enumerate(blended):
        piece = gather_line(piece, token if head == heads - 1 else None)
        blocks += piece + [swap_core(block) for block in piece]
    rest = (blocks, embedded, gain_row, held)

    kept, sent = mlp(3, place, *rest)
    third = add(kept, swap_core(sent))
    inward = along_hid(third, INWARD)
    middle = along_hid(third, MIDDLE)
    kept, sent = mlp(2, after(place, third), *rest)
    moved = swap_core(sent)
    kept_first, sent_first = mlp(1, after(place, kept), *rest)
    second = add(kept, moved, after(inward, kept_first))
    kept, sent, residual = mlp(0, after(place, second), *rest)
    first = add(kept_first, swap_core(sent_first))
    second = along_hid(second, SECOND)
    first = along_hid(first, NEXT)
    total = residual.astype(jnp.float32)
    for piece in (kept, swap_core(sent), middle, first, second):
        total = total + piece.astype(jnp.float32)
    output_rows = total.astype(jnp.bfloat16).reshape(home_cells, 4 * model)

    def project_merged(blocks):
        blocks = blocks + [swap_core(block) for block in blocks]
        return jnp.dot(
            jnp.concatenate(blocks, axis=0), merge_weight, preferred_element_type=jnp.float32
        ).astype(jnp.bfloat16)

    *nearer, third = gather_line(output_rows)
    most = project_merged(nearer)
    last = project_merged([after(third, most)])
    routed = []
    for projected, distances in ((most, (0, 1, 2)), (last, (3,))):
        homes = jnp.stack(
            [2 * (height ^ k) + side for side in (core, 1 - core) for k in distances]
        )
        local = (
            homes[:, None] * home_cells + jnp.arange(home_cells, dtype=jnp.int32)[None, :]
        ).reshape(-1)
        if bands == 4:
            routed += [
                (lax.ppermute(projected, "req", [(i, i ^ shift) for i in range(4)]), band ^ shift, local)
                for shift in (3, 1, 2)
            ]
            routed.append((projected, band, local))
        else:
            every = jnp.arange(bands, dtype=jnp.int32)[:, None] * merged_rows + local[None, :]
            routed.append(
                (lax.all_gather(projected, "req", axis=0, tiled=True), 0, every.reshape(-1))
            )
    returned = jnp.zeros((merged_rows, merge_weight.shape[1]), jnp.float32)
    for piece, piece_band, local in routed:
        merged_index = piece_band * merged_rows + local
        holding = (cell_start[None, :] <= merged_index[:, None]) & (
            merged_index[:, None] < cell_end[None, :]
        )
        holding = holding & (owners == band)[None, :]
        target = jnp.sum(
            jnp.where(holding, merged_index[:, None] + (preceding - cell_start)[None, :] + 1, 0),
            axis=1,
        )
        chosen = (target[None, :] == slots[:, None] + 1).astype(jnp.bfloat16)
        piece = after(piece, last)
        returned = returned + jnp.dot(chosen, piece, preferred_element_type=jnp.float32)
    return returned.astype(jnp.bfloat16)[None]


def solution(mesh):
    return jax.shard_map(
        on_device,
        mesh=mesh,
        in_specs=(
            P("req", None),
            P("req"),
            P(),
            P(),
            P(),
            P(),
            P(),
            P(None, None, "hid"),
            P(),
            P(),
            P(None, "hid"),
            P("hid", None),
            P(None, "hid"),
        ),
        out_specs=P("req", None, "hid"),
        check_vma=False,
    )
```

```python
import functools
import math

import jax
import jax.numpy as jnp
from jax import lax
from jax.experimental import pallas as pl
from jax.experimental.pallas import tpu as pltpu
from jax.sharding import PartitionSpec as P

HEAD_DIM = 88
TILE = 256
LANES = 128
LOW = -1e30
VMEM_LIMIT = 58 * 1024 * 1024
SHARED_VMEM = 24 * 1024 * 1024
ADD_VMEM = 8 * 1024 * 1024

NT = (((1,), (1,)), ((), ()))
TN = (((0,), (0,)), ((), ()))
TT = (((0,), (1,)), ((), ()))


def dot(left, right, dims=(((1,), (0,)), ((), ()))):
    return lax.dot_general(left, right, dims, preferred_element_type=jnp.float32)


def norm_rows(widened, gain_row):
    centered = widened - jnp.mean(widened, axis=-1, keepdims=True)
    variance = jnp.mean(centered * centered, axis=-1, keepdims=True)
    return centered * lax.rsqrt(variance + 1e-06) * gain_row


def whole(shape):
    return pl.BlockSpec(shape, lambda *_: (0,) * len(shape))


def project_kernel(
    base_ref, grid_ref, patches_ref, row_ref, col_ref, gain_ref, weight_ref, embedded_ref, q_ref, *kv_refs
):
    rows = patches_ref.shape[0]
    requests = grid_ref.shape[1]
    across = grid_ref[1:2, :] // 2
    cells = (grid_ref[0:1, :] // 2) * across
    before = lax.broadcasted_iota(jnp.int32, (requests, requests), 0)
    after = lax.broadcasted_iota(jnp.int32, (requests, requests), 1)
    earlier = jnp.where(before < after, 1.0, 0.0).astype(jnp.bfloat16)
    wide = jnp.broadcast_to(cells.astype(jnp.float32), (8, requests)).astype(jnp.bfloat16)
    starts = 4 * dot(wide, earlier)[0:1, :].astype(jnp.int32)
    index = base_ref[0] + pl.program_id(0) * rows
    index = index + lax.broadcasted_iota(jnp.int32, (rows, requests), 0)
    inside = (index >= starts) & (index < starts + 4 * cells)
    offset = jnp.sum(jnp.where(inside, index - starts, 0), axis=1, keepdims=True)
    cells_across = jnp.sum(jnp.where(inside, across, 0), axis=1, keepdims=True)
    shift = jnp.where(cells_across == 16, 4, jnp.where(cells_across == 8, 3, 2))
    block = offset >> 2
    corner = offset & 3
    row_place = 2 * (block >> shift) + (corner >> 1)
    col_place = 2 * (block & (cells_across - 1)) + (corner & 1)
    lane = lax.broadcasted_iota(jnp.int32, (rows, row_ref.shape[0]), 1)
    pick_row = jnp.where(lane == row_place, 1.0, 0.0).astype(jnp.bfloat16)
    pick_col = jnp.where(lane == col_place, 1.0, 0.0).astype(jnp.bfloat16)
    embedded = (
        patches_ref[...].astype(jnp.float32)
        + dot(pick_row, row_ref[...])
        + dot(pick_col, col_ref[...])
    ).astype(jnp.bfloat16)
    embedded_ref[...] = embedded
    normed = norm_rows(embedded.astype(jnp.float32), gain_ref[...]).astype(jnp.bfloat16)
    projected = dot(weight_ref[...], normed, NT).astype(jnp.bfloat16)
    width = q_ref.shape[0]
    q_ref[...] = projected[0:width]
    key_rows = projected[width : 2 * width]
    value_rows = projected[2 * width : 3 * width]
    for head, kv_ref in enumerate(kv_refs):
        span = slice(head * HEAD_DIM, (head + 1) * HEAD_DIM)
        kv_ref[0:HEAD_DIM, :] = key_rows[span]
        kv_ref[HEAD_DIM : 2 * HEAD_DIM, :] = value_rows[span]


def project(base, grid, patches, row_table, col_table, gain, weight):
    rows, model = patches.shape
    width = weight.shape[0] // 3
    return pl.pallas_call(
        project_kernel,
        grid_spec=pltpu.PrefetchScalarGridSpec(
            num_scalar_prefetch=1,
            grid=(rows // 512,),
            in_specs=[
                whole(grid.shape),
                pl.BlockSpec((512, model), lambda i, _: (i, 0)),
                whole(row_table.shape),
                whole(col_table.shape),
                whole(gain.shape),
                whole(weight.shape),
            ],
            out_specs=[
                pl.BlockSpec((512, model), lambda i, _: (i, 0)),
                pl.BlockSpec((width, 512), lambda i, _: (0, i)),
            ]
            + [pl.BlockSpec((2 * HEAD_DIM, 512), lambda i, _: (0, i))] * (width // HEAD_DIM),
        ),
        out_shape=[
            jax.ShapeDtypeStruct((rows, model), jnp.bfloat16),
            jax.ShapeDtypeStruct((width, rows), jnp.bfloat16),
        ]
        + [jax.ShapeDtypeStruct((2 * HEAD_DIM, rows), jnp.bfloat16)] * (width // HEAD_DIM),
        compiler_params=pltpu.CompilerParams(vmem_limit_bytes=VMEM_LIMIT),
        cost_estimate=pl.CostEstimate(
            flops=6 * rows * model * width, bytes_accessed=4 * rows * model, transcendentals=0
        ),
    )(base, grid, patches, row_table, col_table, gain, weight)


def attend_kernel(heads, taken, low_ref, high_ref, base_ref, start_ref, end_ref, q_ref, *rest):
    count = base_ref.shape[0]
    states, rest = rest[: taken * heads], rest[taken * heads :]
    parts, outs = rest[: count * heads], rest[count * heads :]
    rows = q_ref.shape[1]
    scale = math.log2(math.e) / math.sqrt(HEAD_DIM)
    for tile in range(rows // TILE):
        span = slice(tile * TILE, (tile + 1) * TILE)
        start = start_ref[:, span]
        end = end_ref[:, span]
        low = low_ref[tile]
        high = high_ref[tile]
        queries = [q_ref[h * HEAD_DIM : (h + 1) * HEAD_DIM, span] for h in range(heads)]
        if taken:
            carry = tuple(
                tuple(state[:, span] for state in states[taken * h : taken * (h + 1)])
                for h in range(heads)
            )
        else:
            carry = tuple(
                (
                    jnp.full((1, TILE), LOW, jnp.float32),
                    jnp.zeros((1, TILE), jnp.float32),
                    jnp.zeros((HEAD_DIM, TILE), jnp.float32),
                )
                for _ in range(heads)
            )
        for number in range(count):
            base = base_ref[number]
            tiles = rows // TILE
            first = jnp.clip((low - base) // TILE, 0, tiles)
            last = jnp.clip((high - base + TILE - 1) // TILE, 0, tiles)

            def step(place, carry, number=number, base=base, queries=queries, start=start, end=end):
                where = pl.ds(pl.multiple_of(place * TILE, TILE), TILE)
                index = base + place * TILE + lax.broadcasted_iota(jnp.int32, (TILE, TILE), 0)
                allowed = (index >= start) & (index < end)
                new = []
                for h in range(heads):
                    part = parts[count * h + number]
                    top, total, acc = carry[h]
                    scores = dot(part[0:HEAD_DIM, where], queries[h], TN) * scale
                    scores = jnp.where(allowed, scores, LOW)
                    higher = jnp.maximum(top, jnp.max(scores, axis=0, keepdims=True))
                    weights = jnp.exp2(scores - higher)
                    fade = jnp.exp2(top - higher)
                    total = total * fade + jnp.sum(weights, axis=0, keepdims=True)
                    value_rows = part[HEAD_DIM : 2 * HEAD_DIM, where]
                    acc = acc * fade + dot(value_rows, weights.astype(jnp.bfloat16))
                    new.append((higher, total, acc))
                return tuple(new)

            carry = lax.fori_loop(first, last, step, carry)
        for h in range(heads):
            if taken:
                _, total, acc = carry[h]
                outs[h][:, span] = (acc / total).astype(jnp.bfloat16)
            else:
                for out, value in zip(outs[3 * h : 3 * h + 3], carry[h]):
                    out[:, span] = value


def attend(first_head, heads, low, high, bases, start, end, queries, states, parts):
    rows = queries.shape[1]
    smem = pl.BlockSpec(memory_space=pltpu.SMEM)
    if states:
        shapes = [jax.ShapeDtypeStruct((HEAD_DIM, rows), jnp.bfloat16)] * heads
    else:
        shapes = [
            jax.ShapeDtypeStruct((height, rows), jnp.float32) for height in (1, 1, HEAD_DIM)
        ] * heads
    return pl.pallas_call(
        functools.partial(attend_kernel, heads, len(states) // heads),
        grid=(1,),
        in_specs=[smem] * 3
        + [whole(start.shape), whole(end.shape)]
        + [pl.BlockSpec((heads * HEAD_DIM, rows), lambda i: (first_head // heads, 0))]
        + [whole(value.shape) for value in (*states, *parts)],
        out_specs=[whole(x.shape) for x in shapes],
        out_shape=shapes,
        compiler_params=pltpu.CompilerParams(vmem_limit_bytes=VMEM_LIMIT),
        cost_estimate=pl.CostEstimate(
            flops=4 * rows * rows * heads * HEAD_DIM,
            bytes_accessed=8 * rows * heads * HEAD_DIM,
            transcendentals=heads * rows * rows,
        ),
    )(low, high, bases, start, end, queries, *states, *parts)


def load_kernel(*refs):
    stored, held, token_ref, sems = refs[:3], refs[-5:-2], refs[-2], refs[-1]
    copies = [
        pltpu.make_async_copy(source, target, sems.at[i])
        for i, (source, target) in enumerate(zip(stored, held))
    ]
    for copy in copies:
        copy.start()
    token_ref[...] = jnp.zeros(token_ref.shape, token_ref.dtype)
    for copy in copies:
        copy.wait()


def load(stored, marks):
    resident = pl.BlockSpec(memory_space=pltpu.VMEM)
    token = jax.ShapeDtypeStruct((8, LANES), jnp.float32)
    *held, token = pl.pallas_call(
        load_kernel,
        in_specs=[pl.BlockSpec(memory_space=pltpu.HBM)] * 3
        + [pl.BlockSpec(memory_space=pl.ANY)] * len(marks),
        out_specs=[resident] * 4,
        out_shape=[jax.ShapeDtypeStruct(x.shape, x.dtype) for x in stored] + [token],
        scratch_shapes=[pltpu.SemaphoreType.DMA((3,))],
        compiler_params=pltpu.CompilerParams(vmem_limit_bytes=ADD_VMEM),
    )(*stored, *marks)
    return held, token


def mlp_kernel(distance, place_ref, *refs):
    *refs, sems, pieces_ref, rows_ref, blended_ref = refs
    heads = blended_ref.shape[1] // HEAD_DIM
    blocks, refs = refs[: 8 * heads], refs[8 * heads :]
    embedded_ref, gain_ref, out_ref, up_ref, down_ref, kept_ref, sent_ref = refs[:7]
    height, core = place_ref[0], place_ref[1]
    tile = rows_ref.shape[0]
    first_row = pl.multiple_of((height ^ distance) * tile, tile)
    span = pl.ds(first_row, tile)
    copies = [
        pltpu.make_async_copy(block.at[:, span], pieces_ref.at[i], sems.at[i])
        for i, block in enumerate(blocks)
    ]
    copies.append(
        pltpu.make_async_copy(embedded_ref.at[span, :], rows_ref, sems.at[len(blocks)])
    )
    for copy in copies:
        copy.start()
    for copy in copies:
        copy.wait()
    for k in range(4):
        for side in range(2):
            source = 2 * (height ^ k) + (core if side == 0 else 1 - core)
            for h in range(heads):
                where = slice(h * HEAD_DIM, (h + 1) * HEAD_DIM)
                blended_ref[source, where, :] = pieces_ref[8 * h + 4 * side + k]
    blended = blended_ref[...].reshape(-1, tile)
    attended = dot(blended, out_ref[...], TN)
    residual = (rows_ref[...].astype(jnp.float32) + attended).astype(jnp.bfloat16)
    normed = norm_rows(residual.astype(jnp.float32), gain_ref[...]).astype(jnp.bfloat16)
    lifted = dot(normed, up_ref[...])
    activated = (0.5 * lifted * (1.0 + lax.erf(lifted * math.sqrt(0.5)))).astype(jnp.bfloat16)
    partial = dot(activated, down_ref[...]).astype(jnp.bfloat16)
    rows = tile // 2
    for side in range(2):

        @pl.when(core == side)
        def _(side=side):
            mine = slice(side * rows, (side + 1) * rows)
            other = slice((1 - side) * rows, (2 - side) * rows)
            kept_ref[...] = partial[mine]
            sent_ref[...] = partial[other]
            if distance == 0:
                refs[7][...] = residual[mine]


def mlp(distance, place, blocks, embedded, gain, held):
    model = embedded.shape[1]
    heads = len(blocks) // 8
    rows = blocks[0].shape[1] // 4
    hidden = held[1].shape[1]
    away = pl.BlockSpec(memory_space=pltpu.HBM)
    shapes = [jax.ShapeDtypeStruct((rows // 2, model), jnp.bfloat16)] * (2 + (distance == 0))
    return pl.pallas_call(
        functools.partial(mlp_kernel, distance),
        grid=(1,),
        in_specs=[pl.BlockSpec(memory_space=pltpu.SMEM)]
        + [away] * (len(blocks) + 1)
        + [whole(gain.shape)]
        + [pl.BlockSpec(memory_space=pltpu.VMEM)] * 3,
        out_specs=[whole(x.shape) for x in shapes],
        out_shape=shapes,
        scratch_shapes=[
            pltpu.SemaphoreType.DMA((len(blocks) + 1,)),
            pltpu.VMEM((len(blocks), HEAD_DIM, rows), jnp.bfloat16),
            pltpu.VMEM((rows, model), jnp.bfloat16),
            pltpu.VMEM((8, heads * HEAD_DIM, rows), jnp.bfloat16),
        ],
        compiler_params=pltpu.CompilerParams(vmem_limit_bytes=SHARED_VMEM),
        cost_estimate=pl.CostEstimate(
            flops=2 * rows * model * (model + 2 * hidden),
            bytes_accessed=2 * (4 * rows * model + model * (model + 2 * hidden)),
            transcendentals=rows * hidden,
        ),
    )(place, *blocks, embedded, gain, *held)


def add_kernel(*refs):
    total = refs[0][...].astype(jnp.float32)
    for ref in refs[1:-1]:
        total = total + ref[...].astype(jnp.float32)
    refs[-1][...] = total.astype(jnp.bfloat16)


def add(*terms):
    shape = terms[0].shape
    return pl.pallas_call(
        add_kernel,
        grid=(1,),
        in_specs=[whole(shape)] * len(terms),
        out_specs=whole(shape),
        out_shape=jax.ShapeDtypeStruct(shape, jnp.bfloat16),
        compiler_params=pltpu.CompilerParams(vmem_limit_bytes=ADD_VMEM),
        cost_estimate=pl.CostEstimate(
            flops=len(terms) * math.prod(shape),
            bytes_accessed=2 * (len(terms) + 1) * math.prod(shape),
            transcendentals=0,
        ),
    )(*terms)


def after(value, mark):
    return lax.optimization_barrier((value, mark))[0]


def along_hid(value, pairs):
    return lax.ppermute(
        value, "hid", [(2 * a + core, 2 * b + core) for a, b in pairs for core in range(2)]
    )


def swap_core(value):
    return lax.ppermute(value, "hid", [(i, i ^ 1) for i in range(8)])


NEXT = [(0, 1), (1, 0), (2, 3), (3, 2)]
SECOND = [(0, 2), (2, 0), (1, 3), (3, 1)]
MIDDLE = [(1, 2), (2, 1)]
OUTWARD = [(1, 0), (2, 3)]
INWARD = [(0, 1), (3, 2)]


def gather_line(value, mark=None):
    second = along_hid(value, SECOND)
    first = along_hid(value, NEXT)
    passed, kept = (second, after(value, second))
    if mark is not None:
        passed, kept = after(passed, mark), after(kept, mark)
    third = add(along_hid(kept, MIDDLE), along_hid(passed, OUTWARD))
    return [value, first, second, third]


def across_keys(keys, bands):
    if bands == 4:
        return lax.ppermute(keys, "req", [(0, 1), (1, 0), (2, 3), (3, 2)])
    return lax.ppermute(keys, "req", [(i, i + 1) for i in range(bands - 1)])


def along_keys(keys, across, bands):
    if bands == 4:
        return lax.ppermute(across, "req", [(0, 2), (3, 1)])
    return lax.ppermute(keys, "req", [(i + 1, i) for i in range(bands - 1)])


def neighbour_bands(band, bands):
    if bands == 4:
        even = band % 2 == 0
        return jnp.where(even, band + 1, band - 1), jnp.where(even, band - 1, band + 1)
    return band - 1, band + 1


def on_device(
    patches,
    segments,
    grid_sizes,
    owners,
    row_table,
    col_table,
    gain_attn,
    qkv_weight,
    out_weight,
    gain_mlp,
    up_weight,
    down_weight,
    merge_weight,
):
    rows, model = patches.shape
    bands = lax.axis_size("req")
    band = lax.axis_index("req")
    part_count = lax.axis_size("hid")
    requests = grid_sizes.shape[0]

    cells_across = grid_sizes[:, 1] // 2
    cell_count = grid_sizes[:, 0] // 2 * cells_across
    ordinal = jnp.arange(requests, dtype=jnp.int32)
    earlier = ordinal[None, :] < ordinal[:, None]
    cell_start = jnp.sum(jnp.where(earlier, cell_count[None, :], 0), axis=1)
    cell_end = cell_start + cell_count
    same_owner = earlier & (owners[:, None] == owners[None, :])
    preceding = jnp.sum(jnp.where(same_owner, cell_count[None, :], 0), axis=1)

    base = (band * rows).astype(jnp.int32)
    embedded, queries, *keys = project(
        base[None],
        grid_sizes.T,
        patches,
        row_table,
        col_table,
        gain_attn,
        jnp.swapaxes(qkv_weight, 1, 2).reshape(-1, model),
    )

    patch_index = base + jnp.arange(rows, dtype=jnp.int32)
    mine = (4 * cell_start[:, None] <= patch_index[None, :]) & (
        patch_index[None, :] < 4 * cell_end[:, None]
    )
    start = jnp.sum(jnp.where(mine, 4 * cell_start[:, None], 0), axis=0, keepdims=True)
    end = jnp.sum(jnp.where(mine, 4 * cell_end[:, None], 0), axis=0, keepdims=True)
    low = start[0, ::TILE]
    high = end[0, TILE - 1 :: TILE]
    beyond = 1 << 28
    part_bands = jnp.stack(neighbour_bands(band, bands))
    bases = jnp.where((part_bands >= 0) & (part_bands < bands), part_bands * rows, beyond)
    near = [across_keys(own, bands) for own in keys]
    heads = len(keys)
    states = attend(0, heads, low, high, base[None], start, end, queries, (), keys)
    near[0] = after(near[0], states[0])
    far = [along_keys(own, across, bands) for own, across in zip(keys, near)]
    blended = []
    for head in range(heads):
        blended += attend(
            head,
            1,
            low,
            high,
            bases,
            start,
            end,
            queries,
            states[3 * head : 3 * head + 3],
            (near[head], far[head]),
        )

    member = lax.axis_index("hid")
    height, core = member // 2, member % 2
    place = jnp.stack([height, core]).astype(jnp.int32)
    home_cells = rows // (4 * part_count)
    merged_rows = rows // 4
    slots = jnp.arange(merged_rows, dtype=jnp.int32)

    gain_row = gain_mlp[None, :]
    held, token = load((out_weight, up_weight, down_weight), (place, gain_row, blended[0]))
    blocks = []
    for head, piece in enumerate(blended):
        piece = gather_line(piece, token if head == 0 else None)
        blocks += piece + [swap_core(block) for block in piece]
    rest = (blocks, embedded, gain_row, held)

    kept, sent = mlp(3, place, *rest)
    third = add(kept, swap_core(sent))
    inward = along_hid(third, INWARD)
    middle = along_hid(third, MIDDLE)
    kept, sent = mlp(2, after(place, third), *rest)
    moved = swap_core(sent)
    kept_first, sent_first = mlp(1, after(place, kept), *rest)
    second = add(kept, moved, after(inward, kept_first))
    kept, sent, residual = mlp(0, after(place, second), *rest)
    first = add(kept_first, swap_core(sent_first))
    second = along_hid(second, SECOND)
    first = along_hid(first, NEXT)
    total = residual.astype(jnp.float32)
    for piece in (kept, swap_core(sent), middle, first, second):
        total = total + piece.astype(jnp.float32)
    output_rows = total.astype(jnp.bfloat16).reshape(home_cells, 4 * model)

    def project_merged(blocks):
        blocks = blocks + [swap_core(block) for block in blocks]
        return jnp.dot(
            jnp.concatenate(blocks, axis=0), merge_weight, preferred_element_type=jnp.float32
        ).astype(jnp.bfloat16)

    *nearer, third = gather_line(output_rows)
    most = project_merged(nearer)
    last = project_merged([after(third, most)])
    routed = []
    for projected, distances in ((most, (0, 1, 2)), (last, (3,))):
        homes = jnp.stack(
            [2 * (height ^ k) + side for side in (core, 1 - core) for k in distances]
        )
        local = (
            homes[:, None] * home_cells + jnp.arange(home_cells, dtype=jnp.int32)[None, :]
        ).reshape(-1)
        if bands == 4:
            routed += [
                (lax.ppermute(projected, "req", [(i, i ^ shift) for i in range(4)]), band ^ shift, local)
                for shift in (3, 1, 2)
            ]
            routed.append((projected, band, local))
        else:
            every = jnp.arange(bands, dtype=jnp.int32)[:, None] * merged_rows + local[None, :]
            routed.append(
                (lax.all_gather(projected, "req", axis=0, tiled=True), 0, every.reshape(-1))
            )
    returned = jnp.zeros((merged_rows, merge_weight.shape[1]), jnp.float32)
    for piece, piece_band, local in routed:
        merged_index = piece_band * merged_rows + local
        holding = (cell_start[None, :] <= merged_index[:, None]) & (
            merged_index[:, None] < cell_end[None, :]
        )
        holding = holding & (owners == band)[None, :]
        target = jnp.sum(
            jnp.where(holding, merged_index[:, None] + (preceding - cell_start)[None, :] + 1, 0),
            axis=1,
        )
        chosen = (target[None, :] == slots[:, None] + 1).astype(jnp.bfloat16)
        piece = after(piece, last)
        returned = returned + jnp.dot(chosen, piece, preferred_element_type=jnp.float32)
    return returned.astype(jnp.bfloat16)[None]


def solution(mesh):
    return jax.shard_map(
        on_device,
        mesh=mesh,
        in_specs=(
            P("req", None),
            P("req"),
            P(),
            P(),
            P(),
            P(),
            P(),
            P(None, None, "hid"),
            P(),
            P(),
            P(None, "hid"),
            P("hid", None),
            P(None, "hid"),
        ),
        out_specs=P("req", None, "hid"),
        check_vma=False,
    )
```
